256 devices in a mesh: leaf: 64 (over z, x, core), vec: 4 (over y).
Axes of the slice: x: 4, y: 4, z: 8, core: 2. Of those that a mesh axis runs over, the one named last changes fastest.
Arguments:
- vectors: bfloat16 [131072, 512], P('leaf', 'vec'), may hold values from -6 to 6
- leaf_basis: bfloat16 [256, 512, 256], P('leaf'), may hold values from -0.25 to 0.25
- up_leaf: bfloat16 [256, 256, 256], P('leaf'), may hold values from -0.25 to 0.25
- up_mid: bfloat16 [128, 256, 256], P('leaf'), may hold values from -0.25 to 0.25
- top_up: bfloat16 [64, 256, 256], P('leaf'), may hold values from -0.046875 to 0.046875
- top_down: bfloat16 [64, 256, 256], P('leaf'), may hold values from -0.375 to 0.375
- couplings: bfloat16 [16, 256, 256], replicated, may hold values from -0.125 to 0.125
- coupling_top: bfloat16 [256, 256], replicated, may hold values from -0.375 to 0.375
- near_blocks: bfloat16 [256, 5, 512, 512], P('leaf', None, 'vec'), may hold values from -0.125 to 0.125
- far_owner: int32 [3584, 1], replicated, may hold values from 0 to 63; in each aligned block of 56 rows (0 to 55, 56 to 111, ...) at most 2 rows name the same one
- far_pick: int32 [3584], replicated, may hold values from 0 to 3
- far_kind: int32 [3584], P('leaf'), may hold values from 0 to 15
Outputs:
- result: bfloat16 [131072, 512], P('leaf', 'vec')
The draws below stay inside these ranges and needn't reach their ends.
Inputs may be any that keep to these rules, and one draw needn't show every extreme that they name: `far_owner`: among the 56 rows r of one aligned block (the far pairs of one subtree), no subtree is named more than 2 times, and in every draw some block names some subtree exactly 2 times.
All inputs are finite; a program needn't handle non-finite values.
Results may differ from the reference program's by a relative error of at most 0.009.
Values may be sent and summed in bfloat16 or wider, within the bound.
No kernel may reach another device: no remote copies, remote signals or barrier semaphores. Data moves between devices by JAX's collectives and lax.ppermute only.
A program may use at most 128 MiB of HBM per device.

```python
import math
import jax
import jax.numpy as jnp
import numpy as np
from jax import lax

LEAF = 512
RANK = 256
NV = 512
KINDS = 16
NEAR = 5
FAR_LEAF = 8
FAR_MID = 8
FAR_ROOT = 8
LEAVES = 256
MIDS = 128
ROWS = 131072
FAR_DEV = 56
CAP = 2
N_LEAF = 64


def touch_ends(result, own_key, least, high):
    index_at = [jax.random.randint(jax.random.fold_in(own_key, axis), (), 0, length) for axis, length in enumerate(result.shape)]
    widest = result.shape.index(max(result.shape))
    next_to = index_at[:widest] + [(index_at[widest] + 1) % result.shape[widest]] + index_at[widest + 1:]
    return result.at[tuple(index_at)].set(least).at[tuple(next_to)].set(high)


def shard_levels(key, shape, cuts, least, largest):
    level, own = 1.0, jax.random.fold_in(key, 6)
    for axis_at, parts in cuts:
        heights = jnp.exp(jax.random.uniform(jax.random.fold_in(own, axis_at), (parts,), jnp.float32, least / len(cuts), largest / len(cuts)))
        level = level * jnp.repeat(heights, shape[axis_at] // parts).reshape([-1 if axis == axis_at else 1 for axis in range(len(shape))])
    return level


def deal_out(rng, own, number, rows, amount, top, most, lean):
    sequence = jax.random.permutation(rng, amount)
    crowded, common = load_shares(amount, rows * top, most, lean, True), load_shares(amount, rows * top, most, lean, False)
    places = jnp.arange(amount)

    def named(lengths, turn):
        used = int((lengths > 0).sum())
        fixed = max(1, used // 4)
        moved = fixed + (places - fixed + turn * (used - fixed)) % max(1, amount - fixed)
        return jnp.zeros((amount,), jnp.int32).at[sequence[jnp.where(places < fixed, places, moved)]].set(jnp.asarray(lengths, jnp.int32))

    lengths = jnp.where(number % 4 == 0, named(crowded, number // 4), named(common, number - number // 4 - 1))
    mixed = jax.random.permutation(jax.random.fold_in(own, 3), amount)
    donor, receiver = mixed[0:amount // 2 * 2:2], mixed[1:amount // 2 * 2:2]
    margin = jnp.minimum(lengths[donor] - 1, most - lengths[receiver]) // 2
    margin = jnp.where((donor == sequence[0]) | (receiver == sequence[0]) | (lengths[receiver] == 0), 0, jnp.maximum(margin, 0))
    moved = jax.random.randint(jax.random.fold_in(own, 4), (amount // 2,), 0, 1 << 20) % (margin + 1)
    lengths = lengths.at[donor].add(-moved).at[receiver].add(moved)
    members = jnp.searchsorted(jnp.cumsum(lengths), jnp.arange(rows * top), side="right").astype(jnp.int32)
    grid = members.reshape(top, rows).T
    grid = grid[jax.random.permutation(jax.random.fold_in(own, 1), rows)]
    turn = jax.random.randint(jax.random.fold_in(own, 2), (rows, 1), 0, top)
    return jnp.take_along_axis(grid, (jnp.arange(top)[None, :] + turn) % top, axis=1)


def load_shares(count, total, limit, lean, full):
    portions = [(1 << 20) // math.isqrt(standing ** lean) + 1 for standing in range(1, count + 1)]
    largest = limit if full else min(limit, max(-(-total // count), total * portions[0] // sum(portions)))
    least = 1 if total - largest >= count - 1 else 0
    given, rest = [largest] + [least] * (count - 1), total - largest - least * (count - 1)
    while rest > 0:
        candidates = [i for i in range(1, count) if given[i] < largest] or [i for i in range(1, count) if given[i] < limit]
        whole, remaining = sum([portions[i] for i in candidates]), rest
        for i in candidates:
            extra = min(limit - given[i], max(1, remaining * portions[i] // whole), rest)
            given[i] = given[i] + extra
            rest = rest - extra
    return np.array(given)


def noise(key, shape, deviation, limit, shards=(), held_as=jnp.bfloat16):
    drawn = jax.random.normal(key, shape, jnp.float32) * deviation
    if len(shards) > 0:
        drawn = shard_levels(key, shape, shards, -0.22, 0.18) * drawn
    return jnp.clip(drawn, min=-limit, max=limit).astype(held_as)


def setup_inputs(seed: int = 0) -> dict:
    keys = jax.random.split(jax.random.key(seed), 13)
    vectors = noise(keys[0], (ROWS, NV), 1.0, 6.0, ((0, 64), (1, 4)))
    leaf_basis = noise(keys[1], (LEAVES, LEAF, RANK), LEAF ** -0.5, 0.25, ((0, 64),))
    up_leaf = noise(keys[2], (LEAVES, RANK, RANK), (2 * RANK) ** -0.5, 0.25, ((0, 64),))
    up_mid = noise(keys[3], (MIDS, RANK, RANK), (2 * RANK) ** -0.5, 0.25, ((0, 64),))
    top_up = noise(keys[4], (N_LEAF, RANK, RANK), (RANK * N_LEAF) ** -0.5, 0.046875, ((0, 64),))
    top_down = noise(keys[5], (N_LEAF, RANK, RANK), RANK ** -0.5, 0.375, ((0, 64),))
    couplings = noise(keys[6], (KINDS, RANK, RANK), (RANK * FAR_LEAF) ** -0.5, 0.125)
    coupling_top = noise(keys[7], (RANK, RANK), RANK ** -0.5, 0.375)
    near_blocks = noise(keys[8], (LEAVES, NEAR, LEAF, LEAF), (LEAF * NEAR) ** -0.5, 0.125, ((0, 64), (2, 4)))
    far_owner_keys = jax.random.split(jax.random.fold_in(keys[9], 1), (N_LEAF * FAR_DEV) // FAR_DEV)
    far_owner_turns = jax.random.permutation(jax.random.fold_in(keys[9], 3), (N_LEAF * FAR_DEV) // FAR_DEV)
    far_owner = jax.vmap(lambda own, number: deal_out(jax.random.fold_in(keys[9], 2), own, number, FAR_DEV, N_LEAF, 1, CAP, 1))(far_owner_keys, far_owner_turns).reshape((N_LEAF * FAR_DEV, 1))
    far_pick = touch_ends(jax.random.randint(keys[10], (N_LEAF * FAR_DEV,), 0, 4), jax.random.fold_in(keys[10], 1), 0, 3).astype(jnp.int32)
    far_kind = touch_ends(jax.random.randint(keys[11], (N_LEAF * FAR_DEV,), 0, KINDS), jax.random.fold_in(keys[11], 1), 0, KINDS - 1).astype(jnp.int32)
    return dict(vectors=vectors, leaf_basis=leaf_basis, up_leaf=up_leaf, up_mid=up_mid, top_up=top_up, top_down=top_down, couplings=couplings, coupling_top=coupling_top, near_blocks=near_blocks, far_owner=far_owner, far_pick=far_pick, far_kind=far_kind)


def couple(packed, coeff_leaf, coeff_mid, coeff_root, couplings):
    owners, pick_ids, kind_ids = packed
    first_end = 4 * FAR_LEAF
    second_end = first_end + 2 * FAR_MID
    source_leaf = owners[:first_end] * 4 + pick_ids[:first_end] % 4
    source_mid = owners[first_end:second_end] * 2 + pick_ids[first_end:second_end] % 2
    source_root = owners[second_end:]
    partner_coeffs = jnp.concatenate([jnp.take(coeff_leaf, source_leaf, axis=0), jnp.take(coeff_mid, source_mid, axis=0), jnp.take(coeff_root, source_root, axis=0)], axis=0).astype(jnp.float32)
    matrices = jnp.take(couplings, kind_ids, axis=0).astype(jnp.float32)
    products = jnp.einsum('frs,fsv->frv', matrices, partner_coeffs)
    far_leaf = products[:first_end].reshape(4, FAR_LEAF, RANK, NV).sum(axis=1)
    far_mid = products[first_end:second_end].reshape(2, FAR_MID, RANK, NV).sum(axis=1)
    far_root = products[second_end:].reshape(1, FAR_ROOT, RANK, NV).sum(axis=1)
    return far_leaf, far_mid, far_root


def reference(vectors, leaf_basis, up_leaf, up_mid, top_up, top_down, couplings, coupling_top, near_blocks, far_owner, far_pick, far_kind):
    blocked = vectors.reshape(LEAVES, LEAF, NV).astype(jnp.float32)
    coeff_leaf = jnp.einsum('nlr,nlv->nrv', leaf_basis.astype(jnp.float32), blocked).astype(jnp.bfloat16)
    coeff_mid = jnp.einsum('nrs,nrv->nsv', up_leaf.astype(jnp.float32), coeff_leaf.astype(jnp.float32)).reshape(MIDS, 2, RANK, NV).sum(axis=1).astype(jnp.bfloat16)
    coeff_root = jnp.einsum('nrs,nrv->nsv', up_mid.astype(jnp.float32), coeff_mid.astype(jnp.float32)).reshape(N_LEAF, 2, RANK, NV).sum(axis=1).astype(jnp.bfloat16)
    top_coeff = jnp.einsum('nrs,nrv->sv', top_up.astype(jnp.float32), coeff_root.astype(jnp.float32)).astype(jnp.bfloat16)
    top_local = jnp.dot(coupling_top, top_coeff, preferred_element_type=jnp.float32).astype(jnp.bfloat16)
    top_share = jnp.einsum('nrs,sv->nrv', top_down.astype(jnp.float32), top_local.astype(jnp.float32))
    packed = (far_owner.reshape(N_LEAF, FAR_DEV), far_pick.reshape(N_LEAF, FAR_DEV), far_kind.reshape(N_LEAF, FAR_DEV))
    far_leaf, far_mid, far_root = lax.map(lambda item: couple(item, coeff_leaf, coeff_mid, coeff_root, couplings), packed)
    far_leaf = far_leaf.reshape(LEAVES, RANK, NV)
    far_mid = far_mid.reshape(MIDS, RANK, NV)
    far_root = far_root.reshape(N_LEAF, RANK, NV)
    down_root = (far_root + top_share).astype(jnp.bfloat16)
    down_mid = (far_mid + jnp.einsum('nrs,nsv->nrv', up_mid.astype(jnp.float32), jnp.repeat(down_root, 2, axis=0).astype(jnp.float32))).astype(jnp.bfloat16)
    down_leaf = (far_leaf + jnp.einsum('nrs,nsv->nrv', up_leaf.astype(jnp.float32), jnp.repeat(down_mid, 2, axis=0).astype(jnp.float32))).astype(jnp.bfloat16)
    far_field = jnp.einsum('nlr,nrv->nlv', leaf_basis.astype(jnp.float32), down_leaf.astype(jnp.float32))
    halo_rows = (NEAR // 2) * LEAF
    padded = jnp.pad(vectors.astype(jnp.float32), ((halo_rows, halo_rows), (0, 0)))
    near_field = jnp.zeros((LEAVES, LEAF, NV), jnp.float32)
    for offset in range(NEAR):
        window = padded[offset * LEAF: offset * LEAF + ROWS].reshape(LEAVES, LEAF, NV)
        near_field = near_field + jnp.einsum('nil,nlv->niv', near_blocks[:, offset].astype(jnp.float32), window)
    return (far_field + near_field).reshape(ROWS, NV).astype(jnp.bfloat16)
```

```python
import jax
import jax.numpy as jnp
import numpy as np
from jax import lax
from jax.experimental import pallas as pl
from jax.experimental.pallas import tpu as pltpu
from jax.sharding import Mesh
from jax.sharding import PartitionSpec as P

LEAF = 512
RANK = 256
NEAR = 5
FAR_LEAF = 8
FAR_MID = 8
FAR_ROOT = 8
NZ = 8
NX = 4
NY = 4
LEAF_AXES = ("leaf_0", "leaf_1", "leaf_2")
PLANE_AXES = ("leaf_1", "leaf_2")
RING_AXES = ("leaf_0", "leaf_2")
BF16 = jnp.bfloat16
F32 = jnp.float32


def dot(a, b):
    return jnp.dot(a, b, preferred_element_type=F32)


def swap_cores(x):
    return lax.ppermute(x, "leaf_2", [(0, 1), (1, 0)])


def ring_z(x):
    perm = []
    for z in range(NZ):
        perm.append((2 * z, 2 * ((z + 1) % NZ)))
        perm.append((2 * z + 1, 2 * ((z - 1) % NZ) + 1))
    return lax.ppermute(x, RING_AXES, perm)


def shift_y(x, step):
    return lax.ppermute(x, "vec", [(y, (y + step) % NY) for y in range(NY)])


def outer_halo(x):
    count = NZ * NX * 2
    perm = []
    for p in range(count):
        target = p + 1 if p % 2 else p - 1
        if 0 <= target < count:
            perm.append((p, target))
    return lax.ppermute(x, LEAF_AXES, perm)


def pair_list(valid, packed, filler):
    amount = valid.shape[0]
    ids = jnp.arange(amount, dtype=jnp.int32)
    before = jnp.sum(jnp.where(valid[None, :] & (ids[None, :] < ids[:, None]), 1, 0), axis=1)
    place = jnp.where(valid, before, -1)
    count = jnp.sum(valid.astype(jnp.int32))
    listed = jnp.sum(jnp.where(place[None, :] == ids[:, None], packed[None, :], 0), axis=1)
    listed = jnp.where(ids < count, listed, filler)
    return listed.astype(jnp.int32), count.reshape(1).astype(jnp.int32)


UNROLL = 4


def couple_body(nodes, listed, count, coup, own, r1, r2, r3, r4, mine, sib, buf, acc, sem):
    n = nodes
    copies = [
        pltpu.make_async_copy(own, buf.at[0:n], sem.at[0]),
        pltpu.make_async_copy(r1, buf.at[n : 3 * n], sem.at[1]),
        pltpu.make_async_copy(r2, buf.at[3 * n : 5 * n], sem.at[2]),
        pltpu.make_async_copy(r3, buf.at[5 * n : 7 * n], sem.at[3]),
        pltpu.make_async_copy(r4, buf.at[7 * n : 8 * n], sem.at[4]),
    ]
    for c in copies:
        c.start()

    def zero(i, _):
        acc[i] = jnp.zeros((RANK, acc.shape[2]), F32)
        return 0

    lax.fori_loop(0, 8 * n + 1, zero, 0)
    for c in copies:
        c.wait()

    def step(g, _):
        where, parts = [], []
        for u in range(UNROLL):
            e = listed[g * UNROLL + u]
            where.append(e >> 10)
            parts.append(dot(coup[e & 15], buf[(e >> 4) & 63]))
        for t, part in zip(where, parts):
            acc[t] += part
        return 0

    lax.fori_loop(0, (count[0] + UNROLL - 1) // UNROLL, step, 0)

    def out(i, _):
        mine[i] = acc[i].astype(BF16)
        sib[i] = acc[i + 4 * n].astype(BF16)
        return 0

    lax.fori_loop(0, 4 * n, out, 0)


def couple(nodes, listed, count, coup, own, r1, r2, r3, r4):
    width = own.shape[-1]
    shape = jax.ShapeDtypeStruct((4 * nodes, RANK, width), BF16)
    any_spec = pl.BlockSpec(memory_space=pl.ANY)

    def body(*refs):
        couple_body(nodes, *refs)

    return pl.pallas_call(
        body,
        out_shape=(shape, shape),
        in_specs=[
            pl.BlockSpec(memory_space=pltpu.SMEM),
            pl.BlockSpec(memory_space=pltpu.SMEM),
            pl.BlockSpec(memory_space=pltpu.VMEM),
        ]
        + [any_spec] * 5,
        out_specs=(pl.BlockSpec(memory_space=pltpu.VMEM),) * 2,
        scratch_shapes=[
            pltpu.VMEM((8 * nodes, RANK, width), BF16),
            pltpu.VMEM((8 * nodes + 1, RANK, width), F32),
            pltpu.SemaphoreType.DMA((5,)),
        ],
        name=f"couple_{nodes}",
    )(listed, count, coup, own, r1, r2, r3, r4)


def near_body(place, blocks, *refs):
    chunks, out, buf, sem = refs[:8], refs[8], refs[9], refs[10]
    core, y = place[0], place[1]
    copies = []
    for k in range(4):
        outer, inner = chunks[2 * k], chunks[2 * k + 1]
        cols = pl.ds(128 * k, 128)
        copies.append(
            pltpu.make_async_copy(outer.at[0:2048], buf.at[1024:3072, cols], sem.at[3 * k])
        )
        copies.append(
            pltpu.make_async_copy(
                outer.at[2048:3072], buf.at[pl.ds(core * 3072, 1024), cols], sem.at[3 * k + 1]
            )
        )
        copies.append(
            pltpu.make_async_copy(
                inner, buf.at[pl.ds((1 - core) * 3072, 1024), cols], sem.at[3 * k + 2]
            )
        )
    for c in copies:
        c.start()
    for c in copies:
        c.wait()
    targets = [y, (y + 3) % 4, (y + 1) % 4, (y + 2) % 4]
    for i in range(4):
        total = dot(blocks[i, 0], buf[i * LEAF : (i + 1) * LEAF])
        for b in range(1, NEAR):
            total += dot(blocks[i, b], buf[(i + b) * LEAF : (i + b + 1) * LEAF])
        for k in range(4):
            out[targets[k], i] = total[:, 128 * k : 128 * (k + 1)].astype(BF16)


def near_products(place, blocks, chunks):
    any_spec = pl.BlockSpec(memory_space=pl.ANY)
    return pl.pallas_call(
        near_body,
        out_shape=jax.ShapeDtypeStruct((4, 4, 128, 128), BF16),
        in_specs=[pl.BlockSpec(memory_space=pltpu.SMEM), pl.BlockSpec(memory_space=pltpu.VMEM)]
        + [any_spec] * 8,
        out_specs=pl.BlockSpec(memory_space=pltpu.VMEM),
        scratch_shapes=[pltpu.VMEM((4096, 512), BF16), pltpu.SemaphoreType.DMA((12,))],
        name="near",
    )(place, blocks, *chunks)


def tail_body(part_l, part_m, top_local, top_down, up_mid, up_leaf, basis, near, out):
    def far(part, i):
        total = part[0, i].astype(F32)
        for p in range(1, NX):
            total += part[p, i].astype(F32)
        return total

    down_root = (far(part_m, 2) + dot(top_down[0], top_local[...])).astype(BF16)
    for m in range(2):
        down_mid = (far(part_m, m) + dot(up_mid[m], down_root)).astype(BF16)
        for k in range(2):
            i = 2 * m + k
            down_leaf = (far(part_l, i) + dot(up_leaf[i], down_mid)).astype(BF16)
            field = dot(basis[i], down_leaf)
            for v in range(4):
                rows = field[128 * v : 128 * (v + 1)] + near[v, i].astype(F32)
                out[i * LEAF + 128 * v : i * LEAF + 128 * (v + 1)] = rows.astype(BF16)


def tail(part_l, part_m, top_local, top_down, up_mid, up_leaf, basis, near):
    return pl.pallas_call(
        tail_body,
        out_shape=jax.ShapeDtypeStruct((4 * LEAF, part_l.shape[-1]), BF16),
        in_specs=[pl.BlockSpec(memory_space=pltpu.VMEM)] * 8,
        out_specs=pl.BlockSpec(memory_space=pltpu.VMEM),
        name="tail",
    )(part_l, part_m, top_local, top_down, up_mid, up_leaf, basis, near)


def spread(x, axes):
    count = lax.axis_size(axes)
    wide = jnp.broadcast_to(x[None], (count,) + x.shape)
    return lax.all_to_all(wide, axes, split_axis=0, concat_axis=0, tiled=True)


def far_lists(z, x, core, owners, picks, kinds):
    far_rows = owners.shape[1]
    oz, ox, oc = owners // 8, (owners // 2) % 4, owners % 2
    dz = (oz - z) % NZ
    dist = jnp.where(core == 1, dz, (NZ - dz) % NZ)
    other = (oc != core).astype(jnp.int32)
    middle = (dist >= 1) & (dist <= 3)
    held = (ox == x) & (middle | (((dist == 0) | (dist == 4)) & (other == 0)))
    place = jnp.where(dist == 0, 0, jnp.where(dist == 4, 7, 2 * dist - 1 + other))
    device = jnp.arange(8, dtype=jnp.int32)[:, None]
    tx, tc = device // 2, device % 2
    group = jnp.where(tc == core, 0, 4) + tx
    row = jnp.arange(far_rows, dtype=jnp.int32)[None, :]
    first, second = 4 * FAR_LEAF, 4 * FAR_LEAF + 2 * FAR_MID
    leaf_slot = place * 4 + picks % 4
    leaf_target = group * 4 + row // FAR_LEAF
    high_slot = place * 3 + jnp.where(row < second, picks % 2, 2)
    high_target = group * 3 + (row - first) // FAR_MID

    def pack(target, slot):
        return target * 1024 + slot * 16 + kinds

    leaf = pair_list(
        held[:, :first].reshape(-1),
        pack(leaf_target, leaf_slot)[:, :first].reshape(-1),
        32 * 1024,
    )
    high = pair_list(
        held[:, first:].reshape(-1),
        pack(high_target, high_slot)[:, first:].reshape(-1),
        24 * 1024,
    )
    return leaf, high


def gather_ring(own):
    both = jnp.stack([own, swap_cores(own)])
    r1 = ring_z(both)
    r2 = ring_z(r1)
    r3 = ring_z(r2)
    r4 = ring_z(r3[0])
    n = own.shape[0]

    def flat(r):
        return r.reshape((2 * n,) + own.shape[1:])

    return own, flat(r1), flat(r2), flat(r3), r4


def exchange(mine, sib):
    n = mine.shape[0] // NX
    total = mine.astype(F32) + swap_cores(sib).astype(F32)
    total = total.astype(BF16).reshape((NX, n) + mine.shape[1:])
    return lax.all_to_all(total, "leaf_1", split_axis=0, concat_axis=0, tiled=True)


def body(
    vectors,
    leaf_basis,
    up_leaf,
    up_mid,
    top_up,
    top_down,
    couplings,
    coupling_top,
    near_blocks,
    far_owner,
    far_pick,
    far_kind,
):
    z = lax.axis_index("leaf_0")
    x = lax.axis_index("leaf_1")
    core = lax.axis_index("leaf_2")
    y = lax.axis_index("vec")
    width = vectors.shape[1]
    far_rows = far_kind.shape[0]

    coeff_leaf = jnp.einsum(
        "nlr,nlv->nrv", leaf_basis, vectors.reshape(4, LEAF, width), preferred_element_type=F32
    ).astype(BF16)
    mids = jnp.einsum("nrs,nrv->nsv", up_leaf, coeff_leaf, preferred_element_type=F32)
    coeff_mid = mids.reshape(2, 2, RANK, width).sum(axis=1).astype(BF16)
    roots = jnp.einsum("nrs,nrv->nsv", up_mid, coeff_mid, preferred_element_type=F32)
    coeff_root = roots.sum(axis=0, keepdims=True).astype(BF16)
    top_term = jnp.einsum("nrs,nrv->sv", top_up, coeff_root, preferred_element_type=F32)
    coeff_high = jnp.concatenate([coeff_mid, coeff_root], axis=0)

    kinds = spread(far_kind, PLANE_AXES)
    owners = lax.dynamic_slice_in_dim(far_owner.reshape(64, far_rows), z * 8, 8, axis=0)
    picks = lax.dynamic_slice_in_dim(far_pick.reshape(64, far_rows), z * 8, 8, axis=0)
    leaf_list, high_list = far_lists(z, x, core, owners, picks, kinds)

    ring_l = gather_ring(coeff_leaf)
    ring_h = gather_ring(coeff_high)
    part_l = exchange(*couple(4, *leaf_list, couplings, *ring_l))
    part_h = exchange(*couple(3, *high_list, couplings, *ring_h))

    part = lax.all_to_all(
        top_term.reshape(NZ, RANK // NZ, width), "leaf_0", split_axis=0, concat_axis=0, tiled=True
    ).sum(axis=0)
    part = spread(part, PLANE_AXES).sum(axis=0).astype(BF16)
    top_coeff = spread(part, "leaf_0").reshape(RANK, width)
    top_local = dot(coupling_top, top_coeff).astype(BF16)

    outgoing = jnp.where(core == 0, vectors[:1024], vectors[1024:])
    own = jnp.concatenate([vectors, outer_halo(outgoing)], axis=0)
    low = shift_y(own, 1)
    high = shift_y(own, -1)
    half = own.shape[0] // 2
    across = jnp.concatenate([shift_y(low[:half], 1), shift_y(high[half:], -1)], axis=0)
    chunks = []
    for chunk in (own, low, high, across):
        inner = lax.dynamic_slice_in_dim(chunk, 1024 * (1 - core), 1024, axis=0)
        chunks += [chunk, swap_cores(inner)]
    place = jnp.stack([core, y]).astype(jnp.int32)
    products = near_products(place, near_blocks, chunks)
    near = lax.all_to_all(products, "vec", split_axis=0, concat_axis=0, tiled=True)

    return tail(part_l, part_h, top_local, top_down, up_mid, up_leaf, leaf_basis, near)


def solution(mesh):
    torus = Mesh(mesh.devices.reshape(NZ, NX, 2, NY), LEAF_AXES + ("vec",))
    return jax.shard_map(
        body,
        mesh=torus,
        in_specs=(
            P(LEAF_AXES, "vec"),
            P(LEAF_AXES, None, None),
            P(LEAF_AXES, None, None),
            P(LEAF_AXES, None, None),
            P(LEAF_AXES, None, None),
            P(LEAF_AXES, None, None),
            P(),
            P(),
            P(LEAF_AXES, None, "vec", None),
            P(),
            P(),
            P(LEAF_AXES),
        ),
        out_specs=P(LEAF_AXES, "vec"),
        check_vma=False,
    )
```

```python
import jax
import jax.numpy as jnp
from jax import lax
from jax.experimental import pallas as pl
from jax.experimental.pallas import tpu as pltpu
from jax.sharding import Mesh
from jax.sharding import PartitionSpec as P

LEAF = 512
RANK = 256
NEAR = 5
FAR_LEAF = 8
FAR_MID = 8
FAR_ROOT = 8
NZ = 8
NX = 4
NY = 4
LEAF_AXES = ("leaf_0", "leaf_1", "leaf_2")
PLANE_AXES = ("leaf_1", "leaf_2")
RING_AXES = ("leaf_0", "leaf_2")
BF16 = jnp.bfloat16
F32 = jnp.float32


def dot(a, b):
    return jnp.dot(a, b, preferred_element_type=F32)


def swap_cores(x):
    return lax.ppermute(x, "leaf_2", [(0, 1), (1, 0)])


def ring_z(x):
    perm = []
    for z in range(NZ):
        perm.append((2 * z, 2 * ((z + 1) % NZ)))
        perm.append((2 * z + 1, 2 * ((z - 1) % NZ) + 1))
    return lax.ppermute(x, RING_AXES, perm)


def ring_y(x, step=1):
    perm = []
    for y in range(NY):
        perm.append((y, (y + step) % NY))
        perm.append((NY + y, NY + (y - step) % NY))
    return lax.ppermute(x, ("leaf_2", "vec"), perm)


def trade(x, axes):
    return lax.all_to_all(x, axes, split_axis=0, concat_axis=0, tiled=True)


def outer_halo(x):
    count = NZ * NX * 2
    perm = []
    for p in range(count):
        target = p + 1 if p % 2 else p - 1
        if 0 <= target < count:
            perm.append((p, target))
    return lax.ppermute(x, LEAF_AXES, perm)


UNROLL = 4
MIB = 1 << 20


def params(mib):
    return pltpu.CompilerParams(vmem_limit_bytes=mib * MIB)


def lists_body(place, owners, picks, kinds, leaf, high, leaf_base, high_base):
    z, x, core = place[0], place[1], place[2]

    def base(o, _):
        dz = ((o >> 3) - z) & 7
        dist = jnp.where(core == 1, dz, (0 - dz) & 7)
        other = (o & 1) ^ core
        reach = jnp.where(other == 0, 5, 4)
        least = jnp.where(other == 0, 0, 1)
        held = (((o >> 1) & 3) == x) & (dist >= least) & (dist < reach)
        leaf_base[o] = jnp.where(held, 4 * dist + 16 * other, -1)
        high_base[o] = jnp.where(held, 7 * dist + 4 * other - jnp.where(dist > 0, 3, 0), -1)
        return 0

    lax.fori_loop(0, 64, base, 0, unroll=4)
    rows = 4 * FAR_LEAF + 2 * FAR_MID + FAR_ROOT

    def gather(bases, out, first, nodes, mask, extra):
        def node(t, count):
            d, n = t >> 2, t & 3
            start = rows * d + first + 8 * n
            group = (d >> 1) + jnp.where((d & 1) == core, 0, 4)
            target = (4 * group + n) * 1024
            low, add = mask(n), extra(n)
            for j in range(8):
                at = bases[owners[z * 8 * rows + start + j]]
                slot = at + (picks[z * 8 * rows + start + j] & low) + add
                out[count] = target + slot * 16 + kinds[d, first + 8 * n + j]
                count = count + jnp.where(at >= 0, 1, 0)
            return count

        def device(d, count):
            return lax.fori_loop(4 * d, 4 * d + nodes, node, count)

        count = lax.fori_loop(0, 8, device, 0)
        for u in range(UNROLL):
            out[count + u] = 32 * 1024
        out[out.shape[0] - 1] = count

    gather(leaf_base, leaf, 0, 4, lambda n: 3, lambda n: 0)
    gather(
        high_base,
        high,
        4 * FAR_LEAF,
        3,
        lambda n: jnp.where(n < 2, 1, 0),
        lambda n: jnp.where(n < 2, 0, 2),
    )


def pair_lists(*operands):
    smem = pl.BlockSpec(memory_space=pltpu.SMEM)
    return pl.pallas_call(
        lists_body,
        out_shape=(
            jax.ShapeDtypeStruct((384,), jnp.int32),
            jax.ShapeDtypeStruct((256,), jnp.int32),
        ),
        in_specs=[smem] * 4,
        out_specs=(smem, smem),
        scratch_shapes=[pltpu.SMEM((64,), jnp.int32)] * 2,
        compiler_params=params(1),
        name="lists",
    )(*operands)


def couple_body(high, listed, core, coup, *refs):
    ring, (mine, sib, buf, acc, sem) = refs[:-5], refs[-5:]
    copies, start = [], 0
    for i, r in enumerate(ring):
        size = r.shape[0]
        copies.append(pltpu.make_async_copy(r, buf.at[start : start + size], sem.at[i]))
        start += size
    for c in copies:
        c.start()
    count = listed[listed.shape[0] - 1]

    def zero(i, _):
        acc[i] = jnp.zeros((RANK, acc.shape[2]), F32)
        return 0

    lax.fori_loop(0, 33, zero, 0)
    for c in copies:
        c.wait()

    def step(g, _):
        where, parts = [], []
        for u in range(UNROLL):
            e = listed[g * UNROLL + u]
            where.append(e >> 10)
            parts.append(dot(coup[e & 15], buf[(e >> 4) & 63]))
        for t, part in zip(where, parts):
            acc[t] += part
        return 0

    lax.fori_loop(0, (count + UNROLL - 1) // UNROLL, step, 0)
    if high:
        top = buf[7].astype(F32) + buf[14].astype(F32) + buf[21].astype(F32)
        ends = buf[3].astype(F32) + buf[28].astype(F32)
        acc[3] = jnp.where(core[0] == 0, top + ends, top)
        for g in range(1, 8):
            acc[4 * g + 3] = acc[3]

    def out(i, _):
        mine[i] = acc[i].astype(BF16)
        sib[i] = acc[16 + i].astype(BF16)
        return 0

    lax.fori_loop(0, 16, out, 0)


def couple(high, listed, core, coup, *ring):
    width = ring[0].shape[-1]
    slots = sum(r.shape[0] for r in ring)
    any_spec = pl.BlockSpec(memory_space=pl.ANY)
    vmem = pl.BlockSpec(memory_space=pltpu.VMEM)
    smem = pl.BlockSpec(memory_space=pltpu.SMEM)

    def couple_kernel(*refs):
        couple_body(high, *refs)

    return pl.pallas_call(
        couple_kernel,
        out_shape=(jax.ShapeDtypeStruct((16, RANK, width), BF16),) * 2,
        in_specs=[smem, smem, vmem] + [any_spec] * len(ring),
        out_specs=(vmem,) * 2,
        scratch_shapes=[
            pltpu.VMEM((slots, RANK, width), BF16),
            pltpu.VMEM((33, RANK, width), F32),
            pltpu.SemaphoreType.DMA((len(ring),)),
        ],
        compiler_params=params(20),
        name="couple_high" if high else "couple_leaf",
    )(listed, core, coup, *ring)


def near_body(blocks, *refs):
    chunks, outs, (buf, sem) = refs[:4], refs[4:8], refs[8:]
    copies = []
    for k in range(4):
        there = buf.at[:, 128 * k : 128 * (k + 1)]
        copies.append(pltpu.make_async_copy(chunks[k], there, sem.at[k]))
    for c in copies:
        c.start()
    for c in copies:
        c.wait()

    def leaf(i, _):
        total = jnp.zeros((128, 512), F32)
        for b in range(NEAR):
            rows = pl.ds(pl.multiple_of((i + b) * LEAF, LEAF), LEAF)
            total += dot(blocks[i, b], buf[rows])
        for k in range(4):
            outs[k][i] = total[:, 128 * k : 128 * (k + 1)].astype(BF16)
        return 0

    lax.fori_loop(0, 4, leaf, 0)


def near_products(blocks, *chunks):
    any_spec = pl.BlockSpec(memory_space=pl.ANY)
    vmem = pl.BlockSpec(memory_space=pltpu.VMEM)
    return pl.pallas_call(
        near_body,
        out_shape=(jax.ShapeDtypeStruct((4, 128, 128), BF16),) * 4,
        in_specs=[vmem] + [any_spec] * 4,
        out_specs=(vmem,) * 4,
        scratch_shapes=[pltpu.VMEM((4096, 512), BF16), pltpu.SemaphoreType.DMA((4,))],
        compiler_params=params(10),
        name="near",
    )(blocks, *chunks)


def tail_body(place, part_l, part_h, *refs):
    near, (top_c, top_down, up_mid, up_leaf, basis, out, nbuf) = refs[:4], refs[4:]
    core, y = place[2], place[3]
    for k in range(NY):
        nbuf[(y + jnp.where(core == 0, k, 4 - k)) & 3] = near[k][...]

    def far(part, i):
        total = part[0, i].astype(F32)
        for p in range(1, NX):
            total += part[p, i].astype(F32)
        return total

    top_local = dot(top_c[...], far(part_h, 3).astype(BF16)).astype(BF16)
    down_root = (far(part_h, 2) + dot(top_down[0], top_local)).astype(BF16)
    for m in range(2):
        down_mid = (far(part_h, m) + dot(up_mid[m], down_root)).astype(BF16)
        for k in range(2):
            i = 2 * m + k
            down_leaf = (far(part_l, i) + dot(up_leaf[i], down_mid)).astype(BF16)
            field = dot(basis[i], down_leaf)
            for v in range(NY):
                rows = field[128 * v : 128 * (v + 1)] + nbuf[v, i].astype(F32)
                out[i * LEAF + 128 * v : i * LEAF + 128 * (v + 1)] = rows.astype(BF16)


def tail(place, *operands):
    vmem = pl.BlockSpec(memory_space=pltpu.VMEM)
    width = operands[0].shape[-1]
    return pl.pallas_call(
        tail_body,
        out_shape=jax.ShapeDtypeStruct((4 * LEAF, width), BF16),
        in_specs=[pl.BlockSpec(memory_space=pltpu.SMEM)] + [vmem] * len(operands),
        out_specs=vmem,
        scratch_shapes=[pltpu.VMEM((NY, 4, 128, width), BF16)],
        compiler_params=params(12),
        name="tail",
    )(place, *operands)


def exchange(mine, sib):
    got = swap_cores(sib)
    total = (mine.astype(F32) + got.astype(F32)).astype(BF16)
    return trade(total.reshape((NX, 4) + mine.shape[1:]), "leaf_1")


def body(
    vectors,
    leaf_basis,
    up_leaf,
    up_mid,
    top_up,
    top_down,
    couplings,
    coupling_top,
    near_blocks,
    far_owner,
    far_pick,
    far_kind,
):
    z = lax.axis_index("leaf_0")
    x = lax.axis_index("leaf_1")
    core = lax.axis_index("leaf_2")
    y = lax.axis_index("vec")
    width = vectors.shape[1]
    far_rows = far_kind.shape[0]
    core_id = core.reshape(1).astype(jnp.int32)
    place = jnp.stack([z, x, core, y]).astype(jnp.int32)

    coeff_leaf = jnp.einsum(
        "nlr,nlv->nrv", leaf_basis, vectors.reshape(4, LEAF, width), preferred_element_type=F32
    ).astype(BF16)
    mids = jnp.einsum("nrs,nrv->nsv", up_leaf, coeff_leaf, preferred_element_type=F32)
    coeff_mid = mids.reshape(2, 2, RANK, width).sum(axis=1).astype(BF16)
    roots = jnp.einsum("nrs,nrv->nsv", up_mid, coeff_mid, preferred_element_type=F32)
    coeff_root = roots.sum(axis=0, keepdims=True).astype(BF16)
    top_term = jnp.einsum("nrs,nrv->nsv", top_up, coeff_root, preferred_element_type=F32)
    coeff_high = jnp.concatenate([coeff_mid, coeff_root, top_term.astype(BF16)], axis=0)

    other_l = swap_cores(coeff_leaf)
    other_h = swap_cores(coeff_high)
    both_top = (coeff_high[3:].astype(F32) + other_h[3:].astype(F32)).astype(BF16)
    own_high = jnp.concatenate([coeff_high[:3], both_top], axis=0)

    la, lb = [coeff_leaf], [other_l]
    for _ in range(1, 4):
        la.append(ring_z(la[-1]))
        lb.append(ring_z(lb[-1]))
    la.append(ring_z(la[-1]))
    ring_l = la + lb[1:]
    ring_h = [own_high, jnp.concatenate([own_high, other_h[:3]], axis=0)]
    for _ in range(1, 4):
        ring_h.append(ring_z(ring_h[-1]))
    ring_h.append(ring_z(ring_h[-1][:4]))
    del ring_h[1]

    upper = core == 0
    outer = jnp.where(upper, vectors[:1024], vectors[1024:])
    inner = jnp.where(upper, vectors[1024:], vectors[:1024])
    halo = outer_halo(outer)
    sib = swap_cores(inner)
    low, high = jnp.where(upper, halo, sib), jnp.where(upper, sib, halo)
    chunks = [jnp.concatenate([low, vectors, high], axis=0)]
    for _ in range(1, NY):
        chunks.append(ring_y(chunks[-1]))

    kinds = jnp.broadcast_to(far_kind[None], (2 * NX, far_rows))
    kinds = trade(kinds, PLANE_AXES)
    operands = (place, far_owner.reshape(-1), far_pick, kinds)
    leaf_list, high_list = pair_lists(*operands)

    sums_l = couple(False, leaf_list, core_id, couplings, *ring_l)
    sums_h = couple(True, high_list, core_id, couplings, *ring_h)
    part_l = exchange(*sums_l)
    part_h = exchange(*sums_h)

    near = list(near_products(near_blocks, *chunks))
    for k in range(1, NY):
        near[k] = ring_y(near[k], -k)

    return tail(place, part_l, part_h, *near, coupling_top, top_down, up_mid, up_leaf, leaf_basis)


def solution(mesh):
    torus = Mesh(mesh.devices.reshape(NZ, NX, 2, NY), LEAF_AXES + ("vec",))

    return jax.shard_map(
        body,
        mesh=torus,
        in_specs=(
            P(LEAF_AXES, "vec"),
            P(LEAF_AXES, None, None),
            P(LEAF_AXES, None, None),
            P(LEAF_AXES, None, None),
            P(LEAF_AXES, None, None),
            P(LEAF_AXES, None, None),
            P(),
            P(),
            P(LEAF_AXES, None, "vec", None),
            P(),
            P(),
            P(LEAF_AXES),
        ),
        out_specs=P(LEAF_AXES, "vec"),
        check_vma=False,
    )
```

```python
import jax
import jax.numpy as jnp
from jax import lax
from jax.experimental import pallas as pl
from jax.experimental.pallas import tpu as pltpu
from jax.sharding import Mesh
from jax.sharding import PartitionSpec as P

LEAF = 512
RANK = 256
NEAR = 5
FAR_LEAF = 8
FAR_MID = 8
FAR_ROOT = 8
NZ = 8
NX = 4
NY = 4
LEAF_AXES = ("leaf_0", "leaf_1", "leaf_2")
PLANE_AXES = ("leaf_1", "leaf_2")
RING_AXES = ("leaf_0", "leaf_2")
BF16 = jnp.bfloat16
F32 = jnp.float32


def dot(a, b):
    return jnp.dot(a, b, preferred_element_type=F32)


def swap_cores(x):
    return lax.ppermute(x, "leaf_2", [(0, 1), (1, 0)])


def ring_z(x):
    perm = []
    for z in range(NZ):
        perm.append((2 * z, 2 * ((z + 1) % NZ)))
        perm.append((2 * z + 1, 2 * ((z - 1) % NZ) + 1))
    return lax.ppermute(x, RING_AXES, perm)


def ring_y(x, step=1):
    perm = []
    for y in range(NY):
        perm.append((y, (y + step) % NY))
        perm.append((NY + y, NY + (y - step) % NY))
    return lax.ppermute(x, ("leaf_2", "vec"), perm)


def trade(x, axes):
    return lax.all_to_all(x, axes, split_axis=0, concat_axis=0, tiled=True)


def outer_halo(x):
    count = NZ * NX * 2
    perm = []
    for p in range(count):
        target = p + 1 if p % 2 else p - 1
        if 0 <= target < count:
            perm.append((p, target))
    return lax.ppermute(x, LEAF_AXES, perm)


UNROLL = 4
MIB = 1 << 20


def params(mib):
    return pltpu.CompilerParams(vmem_limit_bytes=mib * MIB)


def lists_body(owners, picks, kinds, leaf, high, leaf_base, high_base):
    z, x, core = (lax.axis_index(axis) for axis in LEAF_AXES)

    def base(o, _):
        dz = ((o >> 3) - z) & 7
        dist = jnp.where(core == 1, dz, (0 - dz) & 7)
        other = (o & 1) ^ core
        reach = jnp.where(other == 0, 5, 4)
        least = jnp.where(other == 0, 0, 1)
        held = (((o >> 1) & 3) == x) & (dist >= least) & (dist < reach)
        leaf_base[o] = jnp.where(held, (4 * dist + 16 * other) << 4, -4096)
        high_base[o] = jnp.where(held, (7 * dist + 4 * other) << 4, -4096)
        return 0

    lax.fori_loop(0, 64, base, 0, unroll=8)
    rows = 4 * FAR_LEAF + 2 * FAR_MID + FAR_ROOT

    def gather(bases, out, first, nodes, masks, extras):
        def device(d, count):
            row = rows * d + first
            start = z * 8 * rows + row
            group = (d >> 1) + jnp.where((d & 1) == core, 0, 4)
            for n in range(nodes):
                target = (4 * group + n) * 1024 + extras[n] * 16
                for j in range(8 * n, 8 * n + 8):
                    at = bases[owners[start + j]]
                    pick = (picks[start + j] & masks[n]) << 4 if masks[n] else 0
                    out[count] = at + pick + (target + kinds[d, first + j])
                    count = count + 1 + (at >> 31)
            return count

        count = lax.fori_loop(0, 8, device, 0)
        for u in range(UNROLL):
            out[count + u] = 32 * 1024
        out[out.shape[0] - 1] = count

    gather(leaf_base, leaf, 0, 4, (3, 3, 3, 3), (0, 0, 0, 0))
    gather(high_base, high, 4 * FAR_LEAF, 3, (1, 1, 0), (0, 0, 2))


def pair_lists(*operands):
    smem = pl.BlockSpec(memory_space=pltpu.SMEM)
    return pl.pallas_call(
        lists_body,
        out_shape=(
            jax.ShapeDtypeStruct((384,), jnp.int32),
            jax.ShapeDtypeStruct((256,), jnp.int32),
        ),
        in_specs=[smem] * 3,
        out_specs=(smem, smem),
        scratch_shapes=[pltpu.SMEM((64,), jnp.int32)] * 2,
        compiler_params=params(1),
        name="lists",
    )(*operands)


def couple_body(high, listed, coup, *refs):
    ring, (mine, sib, buf, acc, sem) = refs[:-5], refs[-5:]
    copies, start = [], 0
    for i, r in enumerate(ring):
        size = r.shape[0]
        copies.append(pltpu.make_async_copy(r, buf.at[start : start + size], sem.at[i]))
        start += size
    for c in copies:
        c.start()
    count = listed[listed.shape[0] - 1]

    def zero(i, _):
        acc[i] = jnp.zeros((RANK, acc.shape[2]), F32)
        return 0

    lax.fori_loop(0, 33, zero, 0)
    for c in copies:
        c.wait()

    def step(g, _):
        where, parts = [], []
        for u in range(UNROLL):
            e = listed[g * UNROLL + u]
            where.append(e >> 10)
            parts.append(dot(coup[e & 15], buf[(e >> 4) & 63]))
        for t, part in zip(where, parts):
            acc[t] += part
        return 0

    lax.fori_loop(0, (count + UNROLL - 1) // UNROLL, step, 0)
    if high:
        top = buf[10].astype(F32) + buf[17].astype(F32) + buf[24].astype(F32)
        ends = buf[3].astype(F32) + buf[31].astype(F32)
        acc[3] = jnp.where(lax.axis_index("leaf_2") == 0, top + ends, top)
        for g in range(1, 8):
            acc[4 * g + 3] = acc[3]

    def out(i, _):
        mine[i] = acc[i].astype(BF16)
        sib[i] = acc[16 + i].astype(BF16)
        return 0

    lax.fori_loop(0, 16, out, 0)


def couple(high, listed, coup, *ring):
    width = ring[0].shape[-1]
    slots = sum(r.shape[0] for r in ring)
    any_spec = pl.BlockSpec(memory_space=pl.ANY)
    vmem = pl.BlockSpec(memory_space=pltpu.VMEM)
    smem = pl.BlockSpec(memory_space=pltpu.SMEM)

    def couple_kernel(*refs):
        couple_body(high, *refs)

    return pl.pallas_call(
        couple_kernel,
        out_shape=(jax.ShapeDtypeStruct((16, RANK, width), BF16),) * 2,
        in_specs=[smem, vmem] + [any_spec] * len(ring),
        out_specs=(vmem,) * 2,
        scratch_shapes=[
            pltpu.VMEM((slots, RANK, width), BF16),
            pltpu.VMEM((33, RANK, width), F32),
            pltpu.SemaphoreType.DMA((len(ring),)),
        ],
        compiler_params=params(12),
        name="couple_high" if high else "couple_leaf",
    )(listed, coup, *ring)


def near_body(blocks_hbm, *refs):
    chunks, outs, (buf, blocks, sem) = refs[:4], refs[4:8], refs[8:]
    copies = []
    for k in range(4):
        there = buf.at[:, 128 * k : 128 * (k + 1)]
        copies.append(pltpu.make_async_copy(chunks[k], there, sem.at[k]))
    for i in range(4):
        copies.append(pltpu.make_async_copy(blocks_hbm.at[i], blocks.at[i], sem.at[4 + i]))
    for c in copies:
        c.start()
    for c in copies:
        c.wait()

    def leaf(i, _):
        total = jnp.zeros((128, 512), F32)
        for b in range(NEAR):
            rows = pl.ds(pl.multiple_of((i + b) * LEAF, LEAF), LEAF)
            total += dot(blocks[i, b], buf[rows])
        for k in range(4):
            outs[k][i] = total[:, 128 * k : 128 * (k + 1)].astype(BF16)
        return 0

    lax.fori_loop(0, 4, leaf, 0)


def near_products(blocks, *chunks):
    any_spec = pl.BlockSpec(memory_space=pl.ANY)
    vmem = pl.BlockSpec(memory_space=pltpu.VMEM)
    return pl.pallas_call(
        near_body,
        out_shape=(jax.ShapeDtypeStruct((4, 128, 128), BF16),) * 4,
        in_specs=[pl.BlockSpec(memory_space=pltpu.HBM)] + [any_spec] * 4,
        out_specs=(vmem,) * 4,
        scratch_shapes=[
            pltpu.VMEM((4096, 512), BF16),
            pltpu.VMEM(blocks.shape, BF16),
            pltpu.SemaphoreType.DMA((8,)),
        ],
        compiler_params=params(10),
        name="near",
    )(blocks, *chunks)


def tail_body(part_l, part_h, *refs):
    near, weights, out = refs[:4], refs[4:9], refs[9]
    nbuf, held, sem = refs[10], refs[11:16], refs[16]
    copies = []
    for i in range(5):
        copies.append(pltpu.make_async_copy(weights[i], held[i], sem.at[i]))
    for c in copies:
        c.start()
    top_c, top_down, up_mid, up_leaf, basis = held
    core, y = lax.axis_index("leaf_2"), lax.axis_index("vec")
    for k in range(NY):
        nbuf[(y + jnp.where(core == 0, k, 4 - k)) & 3] = near[k][...]

    def far(part, i):
        total = part[0, i].astype(F32)
        for p in range(1, NX):
            total += part[p, i].astype(F32)
        return total

    for c in copies:
        c.wait()
    top_local = dot(top_c[...], far(part_h, 3).astype(BF16)).astype(BF16)
    down_root = (far(part_h, 2) + dot(top_down[0], top_local)).astype(BF16)
    for m in range(2):
        down_mid = (far(part_h, m) + dot(up_mid[m], down_root)).astype(BF16)
        for k in range(2):
            i = 2 * m + k
            down_leaf = (far(part_l, i) + dot(up_leaf[i], down_mid)).astype(BF16)
            field = dot(basis[i], down_leaf)
            for v in range(NY):
                rows = field[128 * v : 128 * (v + 1)] + nbuf[v, i].astype(F32)
                out[i * LEAF + 128 * v : i * LEAF + 128 * (v + 1)] = rows.astype(BF16)


def tail(*operands):
    vmem, hbm = pl.BlockSpec(memory_space=pltpu.VMEM), pl.BlockSpec(memory_space=pltpu.HBM)
    width = operands[0].shape[-1]
    return pl.pallas_call(
        tail_body,
        out_shape=jax.ShapeDtypeStruct((4 * LEAF, width), BF16),
        in_specs=[vmem] * 6 + [hbm] * 5,
        out_specs=vmem,
        scratch_shapes=[pltpu.VMEM((NY, 4, 128, width), BF16)]
        + [pltpu.VMEM(w.shape, BF16) for w in operands[6:]]
        + [pltpu.SemaphoreType.DMA((5,))],
        compiler_params=params(10),
        name="tail",
    )(*operands)


def pack_body(own, other, out):
    out[0:3] = own[0:3]
    out[3] = (own[3].astype(F32) + other[3].astype(F32)).astype(BF16)
    out[4:7] = other[0:3]


def pack_high(own, other):
    vmem = pl.BlockSpec(memory_space=pltpu.VMEM)
    return pl.pallas_call(
        pack_body,
        out_shape=jax.ShapeDtypeStruct((7,) + own.shape[1:], BF16),
        in_specs=[vmem] * 2,
        out_specs=vmem,
        compiler_params=params(3),
        name="pack",
    )(own, other)


def widen_body(middle, halo, sib, out, sem):
    core = lax.axis_index("leaf_2")
    copies = [
        pltpu.make_async_copy(middle, out.at[1024:3072], sem.at[0]),
        pltpu.make_async_copy(halo, out.at[pl.ds(core * 3072, 1024)], sem.at[1]),
        pltpu.make_async_copy(sib, out.at[pl.ds((1 - core) * 3072, 1024)], sem.at[2]),
    ]
    for c in copies:
        c.start()
    for c in copies:
        c.wait()


def widen(middle, halo, sib):
    any_spec = pl.BlockSpec(memory_space=pl.ANY)
    return pl.pallas_call(
        widen_body,
        out_shape=jax.ShapeDtypeStruct((4096, middle.shape[1]), BF16),
        in_specs=[any_spec] * 3,
        out_specs=pl.BlockSpec(memory_space=pltpu.VMEM),
        scratch_shapes=[pltpu.SemaphoreType.DMA((3,))],
        compiler_params=params(3),
        name="widen",
    )(middle, halo, sib)


def exchange(mine, sib):
    got = swap_cores(sib)
    total = (mine.astype(F32) + got.astype(F32)).astype(BF16)
    return trade(total.reshape((NX, 4) + mine.shape[1:]), "leaf_1")


def body(
    vectors,
    leaf_basis,
    up_leaf,
    up_mid,
    top_up,
    top_down,
    couplings,
    coupling_top,
    near_blocks,
    far_owner,
    far_pick,
    far_kind,
):
    core = lax.axis_index("leaf_2")
    width = vectors.shape[1]
    far_rows = far_kind.shape[0]

    coeff_leaf = jnp.einsum(
        "nlr,nlv->nrv", leaf_basis, vectors.reshape(4, LEAF, width), preferred_element_type=F32
    ).astype(BF16)
    mids = jnp.einsum("nrs,nrv->nsv", up_leaf, coeff_leaf, preferred_element_type=F32)
    coeff_mid = mids.reshape(2, 2, RANK, width).sum(axis=1).astype(BF16)
    roots = jnp.einsum("nrs,nrv->nsv", up_mid, coeff_mid, preferred_element_type=F32)
    coeff_root = roots.sum(axis=0, keepdims=True).astype(BF16)
    top_term = jnp.einsum("nrs,nrv->nsv", top_up, coeff_root, preferred_element_type=F32)
    coeff_high = jnp.concatenate([coeff_mid, coeff_root, top_term.astype(BF16)], axis=0)

    other_l = swap_cores(coeff_leaf)
    other_h = swap_cores(coeff_high)
    la, lb = [coeff_leaf], [other_l]
    for _ in range(1, 4):
        la.append(ring_z(la[-1]))
        lb.append(ring_z(lb[-1]))
    la.append(ring_z(la[-1]))
    ring_l = la + lb[1:]
    ring_h = [pack_high(coeff_high, other_h)]
    for _ in range(1, 4):
        ring_h.append(ring_z(ring_h[-1]))
    ring_h.append(ring_z(ring_h[-1][:4]))

    upper = core == 0
    outer = jnp.where(upper, vectors[:1024], vectors[1024:])
    inner = jnp.where(upper, vectors[1024:], vectors[:1024])
    halo = outer_halo(outer)
    sib = swap_cores(inner)
    chunks = [widen(vectors, halo, sib)]
    for _ in range(1, NY):
        chunks.append(ring_y(chunks[-1]))

    kinds = jnp.broadcast_to(far_kind[None], (2 * NX, far_rows))
    kinds = trade(kinds, PLANE_AXES)
    operands = (far_owner.reshape(-1), far_pick, kinds)
    leaf_list, high_list = pair_lists(*operands)

    sums_l = couple(False, leaf_list, couplings, *ring_l)
    sums_h = couple(True, high_list, couplings, *ring_h)
    part_l = exchange(*sums_l)
    part_h = exchange(*sums_h)

    near = list(near_products(near_blocks, *chunks))
    for k in range(1, NY):
        near[k] = ring_y(near[k], -k)

    return tail(part_l, part_h, *near, coupling_top, top_down, up_mid, up_leaf, leaf_basis)


def solution(mesh):
    torus = Mesh(mesh.devices.reshape(NZ, NX, 2, NY), LEAF_AXES + ("vec",))

    return jax.shard_map(
        body,
        mesh=torus,
        in_specs=(
            P(LEAF_AXES, "vec"),
            P(LEAF_AXES, None, None),
            P(LEAF_AXES, None, None),
            P(LEAF_AXES, None, None),
            P(LEAF_AXES, None, None),
            P(LEAF_AXES, None, None),
            P(),
            P(),
            P(LEAF_AXES, None, "vec", None),
            P(),
            P(),
            P(LEAF_AXES),
        ),
        out_specs=P(LEAF_AXES, "vec"),
        check_vma=False,
    )
```

```python
import jax
import jax.numpy as jnp
from jax import lax
from jax.experimental import pallas as pl
from jax.experimental.pallas import tpu as pltpu
from jax.sharding import Mesh
from jax.sharding import PartitionSpec as P

LEAF = 512
RANK = 256
NEAR = 5
FAR_LEAF = 8
FAR_MID = 8
FAR_ROOT = 8
NZ = 8
NX = 4
NY = 4
LEAF_AXES = ("leaf_0", "leaf_1", "leaf_2")
PLANE_AXES = ("leaf_1", "leaf_2")
RING_AXES = ("leaf_0", "leaf_2")
BF16 = jnp.bfloat16
F32 = jnp.float32


def dot(a, b):
    return jnp.dot(a, b, preferred_element_type=F32)


def swap_cores(x):
    return lax.ppermute(x, "leaf_2", [(0, 1), (1, 0)])


def ring_z(x):
    perm = []
    for z in range(NZ):
        perm.append((2 * z, 2 * ((z + 1) % NZ)))
        perm.append((2 * z + 1, 2 * ((z - 1) % NZ) + 1))
    return lax.ppermute(x, RING_AXES, perm)


def ring_y(x, step=1):
    perm = []
    for y in range(NY):
        perm.append((y, (y + step) % NY))
        perm.append((NY + y, NY + (y - step) % NY))
    return lax.ppermute(x, ("leaf_2", "vec"), perm)


def shift_x(x, step):
    return lax.ppermute(x, "leaf_1", [(i, (i + step) % NX) for i in range(NX)])


def trade(x, axes):
    return lax.all_to_all(x, axes, split_axis=0, concat_axis=0, tiled=True)


def outer_halo(x):
    count = NZ * NX * 2
    perm = []
    for p in range(count):
        target = p + 1 if p % 2 else p - 1
        if 0 <= target < count:
            perm.append((p, target))
    return lax.ppermute(x, LEAF_AXES, perm)


UNROLL = 4
MIB = 1 << 20


def hbm(*arrays):
    return [pltpu.with_memory_space_constraint(a, pltpu.HBM) for a in arrays]


def vmem(*arrays):
    return [pltpu.with_memory_space_constraint(a, pltpu.VMEM) for a in arrays]


def params(mib):
    return pltpu.CompilerParams(vmem_limit_bytes=mib * MIB)


def lists_body(owners, picks, kinds, leaf, high, leaf_base, high_base):
    z, x, core = (lax.axis_index(axis) for axis in LEAF_AXES)

    def base(o, _):
        dz = ((o >> 3) - z) & 7
        dist = jnp.where(core == 1, dz, (0 - dz) & 7)
        other = (o & 1) ^ core
        reach = jnp.where(other == 0, 5, 4)
        least = jnp.where(other == 0, 0, 1)
        held = (((o >> 1) & 3) == x) & (dist >= least) & (dist < reach)
        leaf_base[o] = jnp.where(held, (4 * dist + 16 * other) << 4, -4096)
        high_base[o] = jnp.where(held, (7 * dist + 4 * other) << 4, -4096)
        return 0

    lax.fori_loop(0, 64, base, 0, unroll=8)
    rows = 4 * FAR_LEAF + 2 * FAR_MID + FAR_ROOT

    def gather(bases, out, first, nodes, masks, extras):
        def device(d, count):
            row = rows * d + first
            start = z * 8 * rows + row
            group = (d >> 1) + jnp.where((d & 1) == core, 0, 4)
            for n in range(nodes):
                target = (4 * group + n) * 1024 + extras[n] * 16
                for j in range(8 * n, 8 * n + 8):
                    at = bases[owners[start + j]]
                    pick = (picks[start + j] & masks[n]) << 4 if masks[n] else 0
                    out[count] = at + pick + (target + kinds[d, first + j])
                    count = count + 1 + (at >> 31)
            return count

        count = lax.fori_loop(0, 8, device, 0)
        for u in range(UNROLL):
            out[count + u] = 32 * 1024
        out[out.shape[0] - 1] = count

    gather(leaf_base, leaf, 0, 4, (3, 3, 3, 3), (0, 0, 0, 0))
    gather(high_base, high, 4 * FAR_LEAF, 3, (1, 1, 0), (0, 0, 2))


def pair_lists(*operands):
    smem = pl.BlockSpec(memory_space=pltpu.SMEM)
    return pl.pallas_call(
        lists_body,
        out_shape=(
            jax.ShapeDtypeStruct((384,), jnp.int32),
            jax.ShapeDtypeStruct((256,), jnp.int32),
        ),
        in_specs=[smem] * 3,
        out_specs=(smem, smem),
        scratch_shapes=[pltpu.SMEM((64,), jnp.int32)] * 2,
        compiler_params=params(1),
        name="lists",
    )(*hbm(*operands[:2]), operands[2])


def couple_body(high, listed, coup, *refs):
    ring, (mine, sib, buf, acc, sem) = refs[:-5], refs[-5:]
    copies, start = [], 0
    for i, r in enumerate(ring):
        size = r.shape[0]
        copies.append(pltpu.make_async_copy(r, buf.at[start : start + size], sem.at[i]))
        start += size
    for c in copies:
        c.start()
    count = listed[listed.shape[0] - 1]

    def zero(i, _):
        acc[i] = jnp.zeros((RANK, acc.shape[2]), F32)
        return 0

    lax.fori_loop(0, 33, zero, 0)
    for c in copies:
        c.wait()

    def step(g, _):
        where, parts = [], []
        for u in range(UNROLL):
            e = listed[g * UNROLL + u]
            where.append(e >> 10)
            parts.append(dot(coup[e & 15], buf[(e >> 4) & 63]))
        for t, part in zip(where, parts):
            acc[t] += part
        return 0

    lax.fori_loop(0, (count + UNROLL - 1) // UNROLL, step, 0)
    if high:
        top = buf[10].astype(F32) + buf[17].astype(F32) + buf[24].astype(F32)
        ends = buf[3].astype(F32) + buf[31].astype(F32)
        acc[3] = jnp.where(lax.axis_index("leaf_2") == 0, top + ends, top)
        for g in range(1, 8):
            acc[4 * g + 3] = acc[3]

    def out(i, _):
        mine[i] = acc[i].astype(BF16)
        sib[i] = acc[16 + i].astype(BF16)
        return 0

    lax.fori_loop(0, 16, out, 0)


def couple(high, listed, coup, *ring):
    width = ring[0].shape[-1]
    slots = sum(r.shape[0] for r in ring)
    any_spec = pl.BlockSpec(memory_space=pl.ANY)
    here = pl.BlockSpec(memory_space=pltpu.VMEM)
    smem = pl.BlockSpec(memory_space=pltpu.SMEM)

    def couple_kernel(*refs):
        couple_body(high, *refs)

    return pl.pallas_call(
        couple_kernel,
        out_shape=(jax.ShapeDtypeStruct((16, RANK, width), BF16),) * 2,
        in_specs=[smem, here] + [any_spec] * len(ring),
        out_specs=(here,) * 2,
        scratch_shapes=[
            pltpu.VMEM((slots, RANK, width), BF16),
            pltpu.VMEM((33, RANK, width), F32),
            pltpu.SemaphoreType.DMA((len(ring),)),
        ],
        compiler_params=params(12),
        name="couple_high" if high else "couple_leaf",
    )(*vmem(listed, coup, *ring))


def near_body(blocks_hbm, *refs):
    chunks, outs, (buf, blocks, sem) = refs[:4], refs[4:8], refs[8:]
    copies = []
    for k in range(4):
        there = buf.at[:, 128 * k : 128 * (k + 1)]
        copies.append(pltpu.make_async_copy(chunks[k], there, sem.at[k]))
    for i in range(4):
        copies.append(pltpu.make_async_copy(blocks_hbm.at[i], blocks.at[i], sem.at[4 + i]))
    for c in copies:
        c.start()
    for c in copies:
        c.wait()

    def leaf(i, _):
        total = jnp.zeros((128, 512), F32)
        for b in range(NEAR):
            rows = pl.ds(pl.multiple_of((i + b) * LEAF, LEAF), LEAF)
            total += dot(blocks[i, b], buf[rows])
        for k in range(4):
            outs[k][i] = total[:, 128 * k : 128 * (k + 1)].astype(BF16)
        return 0

    lax.fori_loop(0, 4, leaf, 0)


def near_products(blocks, *chunks):
    any_spec = pl.BlockSpec(memory_space=pl.ANY)
    here = pl.BlockSpec(memory_space=pltpu.VMEM)
    return pl.pallas_call(
        near_body,
        out_shape=(jax.ShapeDtypeStruct((4, 128, 128), BF16),) * 4,
        in_specs=[any_spec] * 5,
        out_specs=(here,) * 4,
        scratch_shapes=[
            pltpu.VMEM((4096, 512), BF16),
            pltpu.VMEM(blocks.shape, BF16),
            pltpu.SemaphoreType.DMA((8,)),
        ],
        compiler_params=params(10),
        name="near",
    )(*hbm(blocks), *vmem(*chunks))


def tail_body(*refs):
    part_l, part_h, near, weights, out = refs[:4], refs[4:8], refs[8:12], refs[12:17], refs[17]
    nbuf, held, sem = refs[18], refs[19:24], refs[24]
    copies = []
    for i in range(5):
        copies.append(pltpu.make_async_copy(weights[i], held[i], sem.at[i]))
    for c in copies:
        c.start()
    top_c, top_down, up_mid, up_leaf, basis = held
    core, y = lax.axis_index("leaf_2"), lax.axis_index("vec")
    for k in range(NY):
        nbuf[(y + jnp.where(core == 0, k, 4 - k)) & 3] = near[k][...]

    def far(part, i):
        total = part[0][i].astype(F32)
        for p in range(1, NX):
            total += part[p][i].astype(F32)
        return total

    for c in copies:
        c.wait()
    top_local = dot(top_c[...], far(part_h, 3).astype(BF16)).astype(BF16)
    down_root = (far(part_h, 2) + dot(top_down[0], top_local)).astype(BF16)
    for m in range(2):
        down_mid = (far(part_h, m) + dot(up_mid[m], down_root)).astype(BF16)
        for k in range(2):
            i = 2 * m + k
            down_leaf = (far(part_l, i) + dot(up_leaf[i], down_mid)).astype(BF16)
            field = dot(basis[i], down_leaf)
            for v in range(NY):
                rows = field[128 * v : 128 * (v + 1)] + nbuf[v, i].astype(F32)
                out[i * LEAF + 128 * v : i * LEAF + 128 * (v + 1)] = rows.astype(BF16)


def tail(*operands):
    here, any_spec = pl.BlockSpec(memory_space=pltpu.VMEM), pl.BlockSpec(memory_space=pl.ANY)
    width = operands[0].shape[-1]
    return pl.pallas_call(
        tail_body,
        out_shape=jax.ShapeDtypeStruct((4 * LEAF, width), BF16),
        in_specs=[here] * 12 + [any_spec] * 5,
        out_specs=here,
        scratch_shapes=[pltpu.VMEM((NY, 4, 128, width), BF16)]
        + [pltpu.VMEM(w.shape, BF16) for w in operands[12:]]
        + [pltpu.SemaphoreType.DMA((5,))],
        compiler_params=params(10),
        name="tail",
    )(*vmem(*operands[:12]), *hbm(*operands[12:]))


def climb_body(leaf, up_leaf, up_mid, top_up, out):
    def lift(up, coeff):
        sides = (((0,), (0,)), ((), ()))
        return lax.dot_general(up, coeff, sides, preferred_element_type=F32)

    root = None
    for m in range(2):
        first, second = lift(up_leaf[2 * m], leaf[2 * m]), lift(up_leaf[2 * m + 1], leaf[2 * m + 1])
        out[m] = (first + second).astype(BF16)
        part = lift(up_mid[m], out[m])
        root = part if m == 0 else root + part
    out[2] = root.astype(BF16)
    out[3] = lift(top_up[0], out[2]).astype(BF16)


def climb(*operands):
    here = pl.BlockSpec(memory_space=pltpu.VMEM)
    return pl.pallas_call(
        climb_body,
        out_shape=jax.ShapeDtypeStruct(operands[0].shape, BF16),
        in_specs=[here] * 4,
        out_specs=here,
        compiler_params=params(6),
        name="climb",
    )(*operands)


def merge_body(mine, got, *outs):
    x = lax.axis_index("leaf_1")
    for g in range(NX):

        def one(i, _):
            at = 4 * ((x + g) & 3) + i
            outs[g][i] = (mine[at].astype(F32) + got[at].astype(F32)).astype(BF16)
            return 0

        lax.fori_loop(0, 4, one, 0)


def merge(mine, got):
    here = pl.BlockSpec(memory_space=pltpu.VMEM)
    return pl.pallas_call(
        merge_body,
        out_shape=(jax.ShapeDtypeStruct((4,) + mine.shape[1:], BF16),) * NX,
        in_specs=[here] * 2,
        out_specs=(here,) * NX,
        compiler_params=params(4),
        name="merge",
    )(*vmem(mine, got))


def head_body(whole, out):
    out[...] = whole[: out.shape[0]]


def first_nodes(whole, count):
    here = pl.BlockSpec(memory_space=pltpu.VMEM)
    return pl.pallas_call(
        head_body,
        out_shape=jax.ShapeDtypeStruct((count,) + whole.shape[1:], BF16),
        in_specs=[here],
        out_specs=here,
        compiler_params=params(2),
        name="first",
    )(*vmem(whole))


def pack_body(own, other, out):
    out[0:3] = own[0:3]
    out[3] = (own[3].astype(F32) + other[3].astype(F32)).astype(BF16)
    out[4:7] = other[0:3]


def pack_high(own, other):
    here = pl.BlockSpec(memory_space=pltpu.VMEM)
    return pl.pallas_call(
        pack_body,
        out_shape=jax.ShapeDtypeStruct((7,) + own.shape[1:], BF16),
        in_specs=[here] * 2,
        out_specs=here,
        compiler_params=params(3),
        name="pack",
    )(*vmem(own, other))


def widen_body(middle, halo, sib, out, sem):
    core = lax.axis_index("leaf_2")
    copies = [
        pltpu.make_async_copy(middle, out.at[1024:3072], sem.at[0]),
        pltpu.make_async_copy(halo, out.at[pl.ds(core * 3072, 1024)], sem.at[1]),
        pltpu.make_async_copy(sib, out.at[pl.ds((1 - core) * 3072, 1024)], sem.at[2]),
    ]
    for c in copies:
        c.start()
    for c in copies:
        c.wait()


def widen(middle, halo, sib):
    any_spec = pl.BlockSpec(memory_space=pl.ANY)
    return pl.pallas_call(
        widen_body,
        out_shape=jax.ShapeDtypeStruct((4096, middle.shape[1]), BF16),
        in_specs=[any_spec] * 3,
        out_specs=pl.BlockSpec(memory_space=pltpu.VMEM),
        scratch_shapes=[pltpu.SemaphoreType.DMA((3,))],
        compiler_params=params(3),
        name="widen",
    )(middle, halo, sib)


def exchange(mine, sib):
    got = swap_cores(sib)
    totals = list(merge(mine, got))
    for g in (2, 1, 3):
        totals[g] = shift_x(totals[g], g)
    return totals


def body(
    vectors,
    leaf_basis,
    up_leaf,
    up_mid,
    top_up,
    top_down,
    couplings,
    coupling_top,
    near_blocks,
    far_owner,
    far_pick,
    far_kind,
):
    core = lax.axis_index("leaf_2")
    width = vectors.shape[1]
    far_rows = far_kind.shape[0]

    coeff_leaf = jnp.einsum(
        "nlr,nlv->nrv", leaf_basis, vectors.reshape(4, LEAF, width), preferred_element_type=F32
    ).astype(BF16)
    coeff_high = climb(coeff_leaf, up_leaf, up_mid, top_up)

    other_l = swap_cores(coeff_leaf)
    other_h = swap_cores(coeff_high)
    la, lb = [coeff_leaf], [other_l]
    for _ in range(1, 4):
        la.append(ring_z(la[-1]))
        lb.append(ring_z(lb[-1]))
    la.append(ring_z(la[-1]))
    ring_l = la + lb[1:]
    ring_h = [pack_high(coeff_high, other_h)]
    for _ in range(1, 4):
        ring_h.append(ring_z(ring_h[-1]))
    ring_h.append(ring_z(first_nodes(ring_h[-1], 4)))

    upper = core == 0
    outer = jnp.where(upper, vectors[:1024], vectors[1024:])
    inner = jnp.where(upper, vectors[1024:], vectors[:1024])
    halo = outer_halo(outer)
    sib = swap_cores(inner)
    chunks = [widen(vectors, halo, sib)]
    for _ in range(1, NY):
        chunks.append(ring_y(chunks[-1]))

    kinds = jnp.broadcast_to(far_kind[None], (2 * NX, far_rows))
    kinds = trade(kinds, PLANE_AXES)
    operands = (far_owner.reshape(-1), far_pick, kinds)
    leaf_list, high_list = pair_lists(*operands)

    sums_l = couple(False, leaf_list, couplings, *ring_l)
    sums_h = couple(True, high_list, couplings, *ring_h)
    part_l = exchange(*sums_l)
    part_h = exchange(*sums_h)

    near = list(near_products(near_blocks, *chunks))
    for k in range(1, NY):
        near[k] = ring_y(near[k], -k)

    return tail(*part_l, *part_h, *near, coupling_top, top_down, up_mid, up_leaf, leaf_basis)


def solution(mesh):
    torus = Mesh(mesh.devices.reshape(NZ, NX, 2, NY), LEAF_AXES + ("vec",))

    return jax.shard_map(
        body,
        mesh=torus,
        in_specs=(
            P(LEAF_AXES, "vec"),
            P(LEAF_AXES, None, None),
            P(LEAF_AXES, None, None),
            P(LEAF_AXES, None, None),
            P(LEAF_AXES, None, None),
            P(LEAF_AXES, None, None),
            P(),
            P(),
            P(LEAF_AXES, None, "vec", None),
            P(),
            P(),
            P(LEAF_AXES),
        ),
        out_specs=P(LEAF_AXES, "vec"),
        check_vma=False,
    )
```

```python
import jax
import jax.numpy as jnp
from jax import lax
from jax.experimental import pallas as pl
from jax.experimental.pallas import tpu as pltpu
from jax.sharding import Mesh
from jax.sharding import PartitionSpec as P

LEAF = 512
RANK = 256
NEAR = 5
FAR_LEAF = 8
FAR_MID = 8
FAR_ROOT = 8
NZ = 8
NX = 4
NY = 4
LEAF_AXES = ("leaf_0", "leaf_1", "leaf_2")
PLANE_AXES = ("leaf_1", "leaf_2")
RING_AXES = ("leaf_0", "leaf_2")
BF16 = jnp.bfloat16
F32 = jnp.float32


def dot(a, b):
    return jnp.dot(a, b, preferred_element_type=F32)


def swap_cores(x):
    return lax.ppermute(x, "leaf_2", [(0, 1), (1, 0)])


def ring_z(x):
    perm = []
    for z in range(NZ):
        perm.append((2 * z, 2 * ((z + 1) % NZ)))
        perm.append((2 * z + 1, 2 * ((z - 1) % NZ) + 1))
    return lax.ppermute(x, RING_AXES, perm)


def ring_y(x, step=1):
    perm = []
    for y in range(NY):
        perm.append((y, (y + step) % NY))
        perm.append((NY + y, NY + (y - step) % NY))
    return lax.ppermute(x, ("leaf_2", "vec"), perm)


def shift_x(x, step):
    return lax.ppermute(x, "leaf_1", [(i, (i + step) % NX) for i in range(NX)])


def trade(x, axes):
    return lax.all_to_all(x, axes, split_axis=0, concat_axis=0, tiled=True)


def outer_halo(x):
    count = NZ * NX * 2
    perm = []
    for p in range(count):
        target = p + 1 if p % 2 else p - 1
        if 0 <= target < count:
            perm.append((p, target))
    return lax.ppermute(x, LEAF_AXES, perm)


UNROLL = 4
MIB = 1 << 20


def hbm(*arrays):
    return [pltpu.with_memory_space_constraint(a, pltpu.HBM) for a in arrays]


def vmem(*arrays):
    return [pltpu.with_memory_space_constraint(a, pltpu.VMEM) for a in arrays]


def params(mib):
    return pltpu.CompilerParams(vmem_limit_bytes=mib * MIB)


def lists_body(owners, picks, kinds, leaf, high, leaf_base, high_base):
    z, x, core = (lax.axis_index(axis) for axis in LEAF_AXES)

    def base(o, _):
        dz = ((o >> 3) - z) & 7
        dist = jnp.where(core == 1, dz, (0 - dz) & 7)
        other = (o & 1) ^ core
        reach = jnp.where(other == 0, 5, 4)
        least = jnp.where(other == 0, 0, 1)
        held = (((o >> 1) & 3) == x) & (dist >= least) & (dist < reach)
        leaf_base[o] = jnp.where(held, (4 * dist + 16 * other) << 4, -4096)
        high_base[o] = jnp.where(held, (7 * dist + 4 * other) << 4, -4096)
        return 0

    lax.fori_loop(0, 64, base, 0, unroll=8)
    rows = 4 * FAR_LEAF + 2 * FAR_MID + FAR_ROOT

    def gather(bases, out, first, nodes, masks, extras):
        def device(d, count):
            row = rows * d + first
            start = z * 8 * rows + row
            group = (d >> 1) + jnp.where((d & 1) == core, 0, 4)
            for n in range(nodes):
                target = (4 * group + n) * 1024 + extras[n] * 16
                for j in range(8 * n, 8 * n + 8):
                    at = bases[owners[0, start + j]]
                    pick = (picks[start + j] & masks[n]) << 4 if masks[n] else 0
                    out[count] = at + pick + (target + kinds[d, first + j])
                    count = count + 1 + (at >> 31)
            return count

        count = lax.fori_loop(0, 8, device, 0)
        for u in range(UNROLL):
            out[count + u] = 32 * 1024
        out[out.shape[0] - 1] = count

    gather(leaf_base, leaf, 0, 4, (3, 3, 3, 3), (0, 0, 0, 0))
    gather(high_base, high, 4 * FAR_LEAF, 3, (1, 1, 0), (0, 0, 2))


def pair_lists(*operands):
    smem = pl.BlockSpec(memory_space=pltpu.SMEM)
    return pl.pallas_call(
        lists_body,
        out_shape=(
            jax.ShapeDtypeStruct((384,), jnp.int32),
            jax.ShapeDtypeStruct((256,), jnp.int32),
        ),
        in_specs=[smem] * 3,
        out_specs=(smem, smem),
        scratch_shapes=[pltpu.SMEM((64,), jnp.int32)] * 2,
        compiler_params=params(1),
        name="lists",
    )(*hbm(*operands[:2]), operands[2])


def couple_body(high, listed, coup, *refs):
    ring, (mine, sib, buf, acc, sem) = refs[:-5], refs[-5:]
    copies, start = [], 0
    for i, r in enumerate(ring):
        size = r.shape[0]
        copies.append(pltpu.make_async_copy(r, buf.at[start : start + size], sem.at[i]))
        start += size
    for c in copies:
        c.start()
    count = listed[listed.shape[0] - 1]

    def zero(i, _):
        acc[i] = jnp.zeros((RANK, acc.shape[2]), F32)
        return 0

    lax.fori_loop(0, 33, zero, 0)
    for c in copies:
        c.wait()

    def step(g, _):
        where, parts = [], []
        for u in range(UNROLL):
            e = listed[g * UNROLL + u]
            where.append(e >> 10)
            parts.append(dot(coup[e & 15], buf[(e >> 4) & 63]))
        for t, part in zip(where, parts):
            acc[t] += part
        return 0

    lax.fori_loop(0, (count + UNROLL - 1) // UNROLL, step, 0)
    if high:
        top = buf[10].astype(F32) + buf[17].astype(F32) + buf[24].astype(F32)
        ends = buf[3].astype(F32) + buf[31].astype(F32)
        acc[3] = jnp.where(lax.axis_index("leaf_2") == 0, top + ends, top)
        for g in range(1, 8):
            acc[4 * g + 3] = acc[3]

    def out(i, _):
        mine[i] = acc[i].astype(BF16)
        sib[i] = acc[16 + i].astype(BF16)
        return 0

    lax.fori_loop(0, 16, out, 0)


def couple(high, listed, coup, *ring):
    width = ring[0].shape[-1]
    slots = sum(r.shape[0] for r in ring)
    any_spec = pl.BlockSpec(memory_space=pl.ANY)
    here = pl.BlockSpec(memory_space=pltpu.VMEM)
    smem = pl.BlockSpec(memory_space=pltpu.SMEM)

    def couple_kernel(*refs):
        couple_body(high, *refs)

    return pl.pallas_call(
        couple_kernel,
        out_shape=(jax.ShapeDtypeStruct((16, RANK, width), BF16),) * 2,
        in_specs=[smem, here] + [any_spec] * len(ring),
        out_specs=(here,) * 2,
        scratch_shapes=[
            pltpu.VMEM((slots, RANK, width), BF16),
            pltpu.VMEM((33, RANK, width), F32),
            pltpu.SemaphoreType.DMA((len(ring),)),
        ],
        compiler_params=params(12),
        name="couple_high" if high else "couple_leaf",
    )(*vmem(listed, coup, *ring))


def near_body(blocks_hbm, *refs):
    chunks, outs, (buf, blocks, sem) = refs[:4], refs[4:8], refs[8:]
    copies = []
    for k in range(4):
        there = buf.at[:, 128 * k : 128 * (k + 1)]
        copies.append(pltpu.make_async_copy(chunks[k], there, sem.at[k]))
    for i in range(4):
        copies.append(pltpu.make_async_copy(blocks_hbm.at[i], blocks.at[i], sem.at[4 + i]))
    for c in copies:
        c.start()
    for c in copies:
        c.wait()

    def leaf(i, _):
        total = jnp.zeros((128, 512), F32)
        for b in range(NEAR):
            rows = pl.ds(pl.multiple_of((i + b) * LEAF, LEAF), LEAF)
            total += dot(blocks[i, b], buf[rows])
        for k in range(4):
            outs[k][i] = total[:, 128 * k : 128 * (k + 1)].astype(BF16)
        return 0

    lax.fori_loop(0, 4, leaf, 0)


def near_products(blocks, *chunks):
    any_spec = pl.BlockSpec(memory_space=pl.ANY)
    here = pl.BlockSpec(memory_space=pltpu.VMEM)
    return pl.pallas_call(
        near_body,
        out_shape=(jax.ShapeDtypeStruct((4, 128, 128), BF16),) * 4,
        in_specs=[any_spec] * 5,
        out_specs=(here,) * 4,
        scratch_shapes=[
            pltpu.VMEM((4096, 512), BF16),
            pltpu.VMEM(blocks.shape, BF16),
            pltpu.SemaphoreType.DMA((8,)),
        ],
        compiler_params=params(10),
        name="near",
    )(*hbm(blocks), *vmem(*chunks))


def tail_body(*refs):
    part_l, part_h, near, weights, out = refs[:4], refs[4:8], refs[8:12], refs[12:17], refs[17]
    nbuf, held, sem = refs[18], refs[19:24], refs[24]
    copies = []
    for i in range(5):
        copies.append(pltpu.make_async_copy(weights[i], held[i], sem.at[i]))
    for c in copies:
        c.start()
    top_c, top_down, up_mid, up_leaf, basis = held
    core, y = lax.axis_index("leaf_2"), lax.axis_index("vec")
    for k in range(NY):
        nbuf[(y + jnp.where(core == 0, k, 4 - k)) & 3] = near[k][...]

    def far(part, i):
        total = part[0][i].astype(F32)
        for p in range(1, NX):
            total += part[p][i].astype(F32)
        return total

    for c in copies:
        c.wait()
    top_local = dot(top_c[...], far(part_h, 3).astype(BF16)).astype(BF16)
    down_root = (far(part_h, 2) + dot(top_down[0], top_local)).astype(BF16)
    for m in range(2):
        down_mid = (far(part_h, m) + dot(up_mid[m], down_root)).astype(BF16)
        for k in range(2):
            i = 2 * m + k
            down_leaf = (far(part_l, i) + dot(up_leaf[i], down_mid)).astype(BF16)
            field = dot(basis[i], down_leaf)
            for v in range(NY):
                rows = field[128 * v : 128 * (v + 1)] + nbuf[v, i].astype(F32)
                out[i * LEAF + 128 * v : i * LEAF + 128 * (v + 1)] = rows.astype(BF16)


def tail(*operands):
    here, any_spec = pl.BlockSpec(memory_space=pltpu.VMEM), pl.BlockSpec(memory_space=pl.ANY)
    width = operands[0].shape[-1]
    return pl.pallas_call(
        tail_body,
        out_shape=jax.ShapeDtypeStruct((4 * LEAF, width), BF16),
        in_specs=[here] * 12 + [any_spec] * 5,
        out_specs=here,
        scratch_shapes=[pltpu.VMEM((NY, 4, 128, width), BF16)]
        + [pltpu.VMEM(w.shape, BF16) for w in operands[12:]]
        + [pltpu.SemaphoreType.DMA((5,))],
        compiler_params=params(10),
        name="tail",
    )(*vmem(*operands[:12]), *hbm(*operands[12:]))


def climb_body(leaf, up_leaf, up_mid, top_up, out):
    def lift(up, coeff):
        sides = (((0,), (0,)), ((), ()))
        return lax.dot_general(up, coeff, sides, preferred_element_type=F32)

    root = None
    for m in range(2):
        first, second = lift(up_leaf[2 * m], leaf[2 * m]), lift(up_leaf[2 * m + 1], leaf[2 * m + 1])
        out[m] = (first + second).astype(BF16)
        part = lift(up_mid[m], out[m])
        root = part if m == 0 else root + part
    out[2] = root.astype(BF16)
    out[3] = lift(top_up[0], out[2]).astype(BF16)


def climb(*operands):
    here = pl.BlockSpec(memory_space=pltpu.VMEM)
    return pl.pallas_call(
        climb_body,
        out_shape=jax.ShapeDtypeStruct(operands[0].shape, BF16),
        in_specs=[here] * 4,
        out_specs=here,
        compiler_params=params(6),
        name="climb",
    )(*vmem(operands[0]), *hbm(*operands[1:]))


def merge_body(mine, got, *outs):
    x = lax.axis_index("leaf_1")
    for g in range(NX):

        def one(i, _):
            at = 4 * ((x + g) & 3) + i
            outs[g][i] = (mine[at].astype(F32) + got[at].astype(F32)).astype(BF16)
            return 0

        lax.fori_loop(0, 4, one, 0)


def merge(mine, got):
    here = pl.BlockSpec(memory_space=pltpu.VMEM)
    return pl.pallas_call(
        merge_body,
        out_shape=(jax.ShapeDtypeStruct((4,) + mine.shape[1:], BF16),) * NX,
        in_specs=[here] * 2,
        out_specs=(here,) * NX,
        compiler_params=params(4),
        name="merge",
    )(*vmem(mine, got))


def head_body(whole, out):
    out[...] = whole[: out.shape[0]]


def first_nodes(whole, count):
    here = pl.BlockSpec(memory_space=pltpu.VMEM)
    return pl.pallas_call(
        head_body,
        out_shape=jax.ShapeDtypeStruct((count,) + whole.shape[1:], BF16),
        in_specs=[here],
        out_specs=here,
        compiler_params=params(2),
        name="first",
    )(*vmem(whole))


def pack_body(own, other, out):
    out[0:3] = own[0:3]
    out[3] = (own[3].astype(F32) + other[3].astype(F32)).astype(BF16)
    out[4:7] = other[0:3]


def pack_high(own, other):
    here = pl.BlockSpec(memory_space=pltpu.VMEM)
    return pl.pallas_call(
        pack_body,
        out_shape=jax.ShapeDtypeStruct((7,) + own.shape[1:], BF16),
        in_specs=[here] * 2,
        out_specs=here,
        compiler_params=params(3),
        name="pack",
    )(own, other)


def widen_body(middle, halo, sib, out, sem):
    core = lax.axis_index("leaf_2")
    copies = [
        pltpu.make_async_copy(middle, out.at[1024:3072], sem.at[0]),
        pltpu.make_async_copy(halo, out.at[pl.ds(core * 3072, 1024)], sem.at[1]),
        pltpu.make_async_copy(sib, out.at[pl.ds((1 - core) * 3072, 1024)], sem.at[2]),
    ]
    for c in copies:
        c.start()
    for c in copies:
        c.wait()


def widen(middle, halo, sib):
    any_spec = pl.BlockSpec(memory_space=pl.ANY)
    return pl.pallas_call(
        widen_body,
        out_shape=jax.ShapeDtypeStruct((4096, middle.shape[1]), BF16),
        in_specs=[any_spec] * 3,
        out_specs=pl.BlockSpec(memory_space=pltpu.VMEM),
        scratch_shapes=[pltpu.SemaphoreType.DMA((3,))],
        compiler_params=params(3),
        name="widen",
    )(middle, halo, sib)


def exchange(mine, sib):
    got = swap_cores(sib)
    totals = list(merge(mine, got))
    for g in (2, 1, 3):
        totals[g] = shift_x(totals[g], g)
    return totals


def body(
    vectors,
    leaf_basis,
    up_leaf,
    up_mid,
    top_up,
    top_down,
    couplings,
    coupling_top,
    near_blocks,
    far_owner,
    far_pick,
    far_kind,
):
    core = lax.axis_index("leaf_2")
    width = vectors.shape[1]
    far_rows = far_kind.shape[0]

    coeff_leaf = jnp.einsum(
        "nlr,nlv->nrv", leaf_basis, vectors.reshape(4, LEAF, width), preferred_element_type=F32
    ).astype(BF16)
    coeff_high = climb(coeff_leaf, up_leaf, up_mid, top_up)

    other_l = swap_cores(coeff_leaf)
    other_h = swap_cores(coeff_high)
    la, lb = [coeff_leaf], [other_l]
    for _ in range(1, 4):
        la.append(ring_z(la[-1]))
        lb.append(ring_z(lb[-1]))
    la.append(ring_z(la[-1]))
    ring_l = la + lb[1:]
    ring_h = [pack_high(coeff_high, other_h)]
    for _ in range(1, 4):
        ring_h.append(ring_z(ring_h[-1]))
    ring_h.append(ring_z(first_nodes(ring_h[-1], 4)))

    upper = core == 0
    outer = jnp.where(upper, vectors[:1024], vectors[1024:])
    inner = jnp.where(upper, vectors[1024:], vectors[:1024])
    halo = outer_halo(outer)
    sib = swap_cores(inner)
    chunks = [widen(vectors, halo, sib)]
    for _ in range(1, NY):
        chunks.append(ring_y(chunks[-1]))

    kinds = jnp.broadcast_to(far_kind[None], (2 * NX, far_rows))
    kinds = trade(kinds, PLANE_AXES)
    operands = (far_owner.reshape(1, -1), far_pick, kinds)
    leaf_list, high_list = pair_lists(*operands)

    sums_l = couple(False, leaf_list, couplings, *ring_l)
    sums_h = couple(True, high_list, couplings, *ring_h)
    part_l = exchange(*sums_l)
    part_h = exchange(*sums_h)

    near = list(near_products(near_blocks, *chunks))
    for k in range(1, NY):
        near[k] = ring_y(near[k], -k)

    return tail(*part_l, *part_h, *near, coupling_top, top_down, up_mid, up_leaf, leaf_basis)


def solution(mesh):
    torus = Mesh(mesh.devices.reshape(NZ, NX, 2, NY), LEAF_AXES + ("vec",))

    return jax.shard_map(
        body,
        mesh=torus,
        in_specs=(
            P(LEAF_AXES, "vec"),
            P(LEAF_AXES, None, None),
            P(LEAF_AXES, None, None),
            P(LEAF_AXES, None, None),
            P(LEAF_AXES, None, None),
            P(LEAF_AXES, None, None),
            P(),
            P(),
            P(LEAF_AXES, None, "vec", None),
            P(),
            P(),
            P(LEAF_AXES),
        ),
        out_specs=P(LEAF_AXES, "vec"),
        check_vma=False,
    )
```

```python
import jax
import jax.numpy as jnp
from jax import lax
from jax.experimental import pallas as pl
from jax.experimental.pallas import tpu as pltpu
from jax.sharding import Mesh
from jax.sharding import PartitionSpec as P

LEAF = 512
RANK = 256
NEAR = 5
FAR_LEAF = 8
FAR_MID = 8
FAR_ROOT = 8
NZ = 8
NX = 4
NY = 4
LEAF_AXES = ("leaf_0", "leaf_1", "leaf_2")
RING_AXES = ("leaf_0", "leaf_2")
BF16 = jnp.bfloat16
F32 = jnp.float32


def dot(a, b):
    return jnp.dot(a, b, preferred_element_type=F32)


def swap_cores(x):
    return lax.ppermute(x, "leaf_2", [(0, 1), (1, 0)])


def ring_z(x):
    perm = []
    for z in range(NZ):
        perm.append((2 * z, 2 * ((z + 1) % NZ)))
        perm.append((2 * z + 1, 2 * ((z - 1) % NZ) + 1))
    return lax.ppermute(x, RING_AXES, perm)


def ring_y(x, step=1):
    perm = []
    for y in range(NY):
        perm.append((y, (y + step) % NY))
        perm.append((NY + y, NY + (y - step) % NY))
    return lax.ppermute(x, ("leaf_2", "vec"), perm)


def shift_x(x, step):
    return lax.ppermute(x, "leaf_1", [(i, (i + step) % NX) for i in range(NX)])


def outer_halo(x):
    count = NZ * NX * 2
    perm = []
    for p in range(count):
        target = p + 1 if p % 2 else p - 1
        if 0 <= target < count:
            perm.append((p, target))
    return lax.ppermute(x, LEAF_AXES, perm)


UNROLL = 4
MIB = 1 << 20


def hbm(*arrays):
    return [pltpu.with_memory_space_constraint(a, pltpu.HBM) for a in arrays]


def vmem(*arrays):
    return [pltpu.with_memory_space_constraint(a, pltpu.VMEM) for a in arrays]


def params(mib):
    return pltpu.CompilerParams(vmem_limit_bytes=mib * MIB)


def lists_body(owners, picks, *refs):
    kinds, (leaf, high, leaf_base, high_base) = refs[:NX], refs[NX:]
    z, x, core = (lax.axis_index(axis) for axis in LEAF_AXES)

    def base(o, _):
        dz = ((o >> 3) - z) & 7
        dist = jnp.where(core == 1, dz, (0 - dz) & 7)
        other = (o & 1) ^ core
        reach = jnp.where(other == 0, 5, 4)
        least = jnp.where(other == 0, 0, 1)
        held = (((o >> 1) & 3) == x) & (dist >= least) & (dist < reach)
        leaf_base[o] = jnp.where(held, (8 * dist + 4 * other) << 4, -4096)
        high_base[o] = jnp.where(held, (7 * dist + 4 * other) << 4, -4096)
        return 0

    lax.fori_loop(0, 64, base, 0, unroll=8)
    rows = 4 * FAR_LEAF + 2 * FAR_MID + FAR_ROOT

    def gather(bases, out, first, nodes, leaves):
        count = jnp.int32(0)
        for s in range(NX):
            tx = (x - s) & 3
            for b in range(2):
                start = (z * 8 + tx * 2 + (core ^ b)) * rows + first
                group = 4 * (tx + 4 * b)

                def node(n, count):
                    low = 3 if leaves else jnp.where(n < 2, 1, 0)
                    extra = 0 if leaves else jnp.where(n < 2, 0, 32)
                    target = (group + n) * 1024 + extra
                    for j in range(8):
                        at = bases[owners[0, start + 8 * n + j]]
                        pick = (picks[start + 8 * n + j] & low) << 4
                        out[count] = at + pick + (target + kinds[s][b, first + 8 * n + j])
                        count = count + 1 + (at >> 31)
                    return count

                count = lax.fori_loop(0, nodes, node, count)
        for u in range(UNROLL):
            out[count + u] = 32 * 1024
        out[out.shape[0] - 1] = count

    gather(leaf_base, leaf, 0, 4, True)
    gather(high_base, high, 4 * FAR_LEAF, 3, False)


def pair_lists(owners, picks, *kinds):
    smem = pl.BlockSpec(memory_space=pltpu.SMEM)
    return pl.pallas_call(
        lists_body,
        out_shape=(
            jax.ShapeDtypeStruct((384,), jnp.int32),
            jax.ShapeDtypeStruct((256,), jnp.int32),
        ),
        in_specs=[smem] * (2 + NX),
        out_specs=(smem, smem),
        scratch_shapes=[pltpu.SMEM((64,), jnp.int32)] * 2,
        compiler_params=params(1),
        name="lists",
    )(*hbm(owners, picks), *kinds)


def couple_body(high, listed, coup, *refs):
    ring, (mine, sib, buf, acc, sem) = refs[:-5], refs[-5:]
    copies, start = [], 0
    for i, r in enumerate(ring):
        size = r.shape[0]
        copies.append(pltpu.make_async_copy(r, buf.at[start : start + size], sem.at[i]))
        start += size
    for c in copies:
        c.start()
    count = listed[listed.shape[0] - 1]

    def zero(i, _):
        acc[i] = jnp.zeros((RANK, acc.shape[2]), F32)
        return 0

    lax.fori_loop(0, 33, zero, 0)
    for c in copies:
        c.wait()

    def step(g, _):
        where, parts = [], []
        for u in range(UNROLL):
            e = listed[g * UNROLL + u]
            where.append(e >> 10)
            parts.append(dot(coup[e & 15], buf[(e >> 4) & 63]))
        for t, part in zip(where, parts):
            acc[t] += part
        return 0

    lax.fori_loop(0, (count + UNROLL - 1) // UNROLL, step, 0)
    if high:
        top = buf[10].astype(F32) + buf[17].astype(F32) + buf[24].astype(F32)
        ends = buf[3].astype(F32) + buf[31].astype(F32)
        acc[3] = jnp.where(lax.axis_index("leaf_2") == 0, top + ends, top)
        for g in range(1, 8):
            acc[4 * g + 3] = acc[3]

    def out(i, _):
        mine[i] = acc[i].astype(BF16)
        sib[i] = acc[16 + i].astype(BF16)
        return 0

    lax.fori_loop(0, 16, out, 0)


def couple(high, listed, coup, *ring):
    width = ring[0].shape[-1]
    slots = sum(r.shape[0] for r in ring)
    any_spec = pl.BlockSpec(memory_space=pl.ANY)
    here = pl.BlockSpec(memory_space=pltpu.VMEM)
    smem = pl.BlockSpec(memory_space=pltpu.SMEM)

    def couple_kernel(*refs):
        couple_body(high, *refs)

    return pl.pallas_call(
        couple_kernel,
        out_shape=(jax.ShapeDtypeStruct((16, RANK, width), BF16),) * 2,
        in_specs=[smem, here] + [any_spec] * len(ring),
        out_specs=(here,) * 2,
        scratch_shapes=[
            pltpu.VMEM((slots, RANK, width), BF16),
            pltpu.VMEM((33, RANK, width), F32),
            pltpu.SemaphoreType.DMA((len(ring),)),
        ],
        compiler_params=params(12),
        name="couple_high" if high else "couple_leaf",
    )(*vmem(listed, coup, *ring))


def near_body(blocks_hbm, *refs):
    chunks, outs, (buf, blocks, sem) = refs[:4], refs[4:8], refs[8:]
    copies = []
    for k in range(4):
        there = buf.at[:, 128 * k : 128 * (k + 1)]
        copies.append(pltpu.make_async_copy(chunks[k], there, sem.at[k]))
    for i in range(4):
        copies.append(pltpu.make_async_copy(blocks_hbm.at[i], blocks.at[i], sem.at[4 + i]))
    for c in copies:
        c.start()
    for c in copies:
        c.wait()

    def leaf(i, _):
        total = jnp.zeros((128, 512), F32)
        for b in range(NEAR):
            rows = pl.ds(pl.multiple_of((i + b) * LEAF, LEAF), LEAF)
            total += dot(blocks[i, b], buf[rows])
        for k in range(4):
            outs[k][i] = total[:, 128 * k : 128 * (k + 1)].astype(BF16)
        return 0

    lax.fori_loop(0, 4, leaf, 0)


def near_products(blocks, *chunks):
    any_spec = pl.BlockSpec(memory_space=pl.ANY)
    here = pl.BlockSpec(memory_space=pltpu.VMEM)
    return pl.pallas_call(
        near_body,
        out_shape=(jax.ShapeDtypeStruct((4, 128, 128), BF16),) * 4,
        in_specs=[any_spec] * 5,
        out_specs=(here,) * 4,
        scratch_shapes=[
            pltpu.VMEM((4096, 512), BF16),
            pltpu.VMEM(blocks.shape, BF16),
            pltpu.SemaphoreType.DMA((8,)),
        ],
        compiler_params=params(10),
        name="near",
    )(*hbm(blocks), *vmem(*chunks))


def tail_body(*refs):
    part_l, part_h, near, weights, out = refs[:4], refs[4:8], refs[8:12], refs[12:17], refs[17]
    nbuf, held, sem = refs[18], refs[19:24], refs[24]
    copies = []
    for i in range(5):
        copies.append(pltpu.make_async_copy(weights[i], held[i], sem.at[i]))
    for c in copies:
        c.start()
    top_c, top_down, up_mid, up_leaf, basis = held
    core, y = lax.axis_index("leaf_2"), lax.axis_index("vec")
    for k in range(NY):
        nbuf[(y + jnp.where(core == 0, k, 4 - k)) & 3] = near[k][...]

    def far(part, i):
        total = part[0][i].astype(F32)
        for p in range(1, NX):
            total += part[p][i].astype(F32)
        return total

    for c in copies:
        c.wait()
    top_local = dot(top_c[...], far(part_h, 3).astype(BF16)).astype(BF16)
    down_root = (far(part_h, 2) + dot(top_down[0], top_local)).astype(BF16)
    for m in range(2):
        down_mid = (far(part_h, m) + dot(up_mid[m], down_root)).astype(BF16)
        for k in range(2):
            i = 2 * m + k
            down_leaf = (far(part_l, i) + dot(up_leaf[i], down_mid)).astype(BF16)
            field = dot(basis[i], down_leaf)
            for v in range(NY):
                rows = field[128 * v : 128 * (v + 1)] + nbuf[v, i].astype(F32)
                out[i * LEAF + 128 * v : i * LEAF + 128 * (v + 1)] = rows.astype(BF16)


def tail(*operands):
    here, any_spec = pl.BlockSpec(memory_space=pltpu.VMEM), pl.BlockSpec(memory_space=pl.ANY)
    width = operands[0].shape[-1]
    return pl.pallas_call(
        tail_body,
        out_shape=jax.ShapeDtypeStruct((4 * LEAF, width), BF16),
        in_specs=[here] * 12 + [any_spec] * 5,
        out_specs=here,
        scratch_shapes=[pltpu.VMEM((NY, 4, 128, width), BF16)]
        + [pltpu.VMEM(w.shape, BF16) for w in operands[12:]]
        + [pltpu.SemaphoreType.DMA((5,))],
        compiler_params=params(10),
        name="tail",
    )(*vmem(*operands[:12]), *hbm(*operands[12:]))


def climb_body(leaf, up_leaf, up_mid, top_up, out):
    def lift(up, coeff):
        sides = (((0,), (0,)), ((), ()))
        return lax.dot_general(up, coeff, sides, preferred_element_type=F32)

    root = None
    for m in range(2):
        first, second = lift(up_leaf[2 * m], leaf[2 * m]), lift(up_leaf[2 * m + 1], leaf[2 * m + 1])
        out[m] = (first + second).astype(BF16)
        part = lift(up_mid[m], out[m])
        root = part if m == 0 else root + part
    out[2] = root.astype(BF16)
    out[3] = lift(top_up[0], out[2]).astype(BF16)


def climb(*operands):
    here = pl.BlockSpec(memory_space=pltpu.VMEM)
    return pl.pallas_call(
        climb_body,
        out_shape=jax.ShapeDtypeStruct(operands[0].shape, BF16),
        in_specs=[here] * 4,
        out_specs=here,
        compiler_params=params(6),
        name="climb",
    )(*vmem(operands[0]), *hbm(*operands[1:]))


def merge_body(mine, got, *outs):
    x = lax.axis_index("leaf_1")
    for g in range(NX):

        def one(i, _):
            at = 4 * ((x + g) & 3) + i
            outs[g][i] = (mine[at].astype(F32) + got[at].astype(F32)).astype(BF16)
            return 0

        lax.fori_loop(0, 4, one, 0)


def merge(mine, got):
    here = pl.BlockSpec(memory_space=pltpu.VMEM)
    return pl.pallas_call(
        merge_body,
        out_shape=(jax.ShapeDtypeStruct((4,) + mine.shape[1:], BF16),) * NX,
        in_specs=[here] * 2,
        out_specs=(here,) * NX,
        compiler_params=params(4),
        name="merge",
    )(*vmem(mine, got))


def head_body(whole, out):
    out[...] = whole[: out.shape[0]]


def first_nodes(whole, count):
    here = pl.BlockSpec(memory_space=pltpu.VMEM)
    return pl.pallas_call(
        head_body,
        out_shape=jax.ShapeDtypeStruct((count,) + whole.shape[1:], BF16),
        in_specs=[here],
        out_specs=here,
        compiler_params=params(2),
        name="first",
    )(*vmem(whole))


def pack_body(own, other, out):
    out[0:3] = own[0:3]
    out[3] = (own[3].astype(F32) + other[3].astype(F32)).astype(BF16)
    out[4:7] = other[0:3]


def join_body(own, other, out):
    out[0:4] = own[...]
    out[4:8] = other[...]


def pack_leaf(own, other):
    here = pl.BlockSpec(memory_space=pltpu.VMEM)
    return pl.pallas_call(
        join_body,
        out_shape=jax.ShapeDtypeStruct((8,) + own.shape[1:], BF16),
        in_specs=[here] * 2,
        out_specs=here,
        compiler_params=params(3),
        name="join",
    )(own, other)


def pack_high(own, other):
    here = pl.BlockSpec(memory_space=pltpu.VMEM)
    return pl.pallas_call(
        pack_body,
        out_shape=jax.ShapeDtypeStruct((7,) + own.shape[1:], BF16),
        in_specs=[here] * 2,
        out_specs=here,
        compiler_params=params(3),
        name="pack",
    )(own, other)


def widen_body(middle, halo, sib, out, sem):
    core = lax.axis_index("leaf_2")
    copies = [
        pltpu.make_async_copy(middle, out.at[1024:3072], sem.at[0]),
        pltpu.make_async_copy(halo, out.at[pl.ds(core * 3072, 1024)], sem.at[1]),
        pltpu.make_async_copy(sib, out.at[pl.ds((1 - core) * 3072, 1024)], sem.at[2]),
    ]
    for c in copies:
        c.start()
    for c in copies:
        c.wait()


def widen(middle, halo, sib):
    any_spec = pl.BlockSpec(memory_space=pl.ANY)
    return pl.pallas_call(
        widen_body,
        out_shape=jax.ShapeDtypeStruct((4096, middle.shape[1]), BF16),
        in_specs=[any_spec] * 3,
        out_specs=pl.BlockSpec(memory_space=pltpu.VMEM),
        scratch_shapes=[pltpu.SemaphoreType.DMA((3,))],
        compiler_params=params(3),
        name="widen",
    )(middle, halo, sib)


def exchange(mine, sib):
    got = swap_cores(sib)
    totals = list(merge(mine, got))
    for g in (2, 1, 3):
        totals[g] = shift_x(totals[g], g)
    return totals


def body(
    vectors,
    leaf_basis,
    up_leaf,
    up_mid,
    top_up,
    top_down,
    couplings,
    coupling_top,
    near_blocks,
    far_owner,
    far_pick,
    far_kind,
):
    core = lax.axis_index("leaf_2")
    width = vectors.shape[1]
    far_rows = far_kind.shape[0]

    coeff_leaf = jnp.einsum(
        "nlr,nlv->nrv", leaf_basis, vectors.reshape(4, LEAF, width), preferred_element_type=F32
    ).astype(BF16)
    coeff_high = climb(coeff_leaf, up_leaf, up_mid, top_up)

    other_l = swap_cores(coeff_leaf)
    other_h = swap_cores(coeff_high)
    ring_l = [pack_leaf(coeff_leaf, other_l)]
    for _ in range(1, 4):
        ring_l.append(ring_z(ring_l[-1]))
    ring_l.append(ring_z(first_nodes(ring_l[-1], 4)))
    ring_h = [pack_high(coeff_high, other_h)]
    for _ in range(1, 4):
        ring_h.append(ring_z(ring_h[-1]))
    ring_h.append(ring_z(first_nodes(ring_h[-1], 4)))

    upper = core == 0
    outer = jnp.where(upper, vectors[:1024], vectors[1024:])
    inner = jnp.where(upper, vectors[1024:], vectors[:1024])
    halo = outer_halo(outer)
    sib = swap_cores(inner)
    chunks = [widen(vectors, halo, sib)]
    for _ in range(1, NY):
        chunks.append(ring_y(chunks[-1]))

    kinds = far_kind.reshape(1, far_rows)
    kinds = [jnp.concatenate([kinds, swap_cores(kinds)], axis=0)]
    for k in range(1, NX):
        kinds.append(shift_x(kinds[0], k))
    operands = (far_owner.reshape(1, -1), far_pick, *kinds)
    leaf_list, high_list = pair_lists(*operands)

    sums_l = couple(False, leaf_list, couplings, *ring_l)
    sums_h = couple(True, high_list, couplings, *ring_h)
    part_l = exchange(*sums_l)
    part_h = exchange(*sums_h)

    near = list(near_products(near_blocks, *chunks))
    for k in range(1, NY):
        near[k] = ring_y(near[k], -k)

    return tail(*part_l, *part_h, *near, coupling_top, top_down, up_mid, up_leaf, leaf_basis)


def solution(mesh):
    torus = Mesh(mesh.devices.reshape(NZ, NX, 2, NY), LEAF_AXES + ("vec",))

    return jax.shard_map(
        body,
        mesh=torus,
        in_specs=(
            P(LEAF_AXES, "vec"),
            P(LEAF_AXES, None, None),
            P(LEAF_AXES, None, None),
            P(LEAF_AXES, None, None),
            P(LEAF_AXES, None, None),
            P(LEAF_AXES, None, None),
            P(),
            P(),
            P(LEAF_AXES, None, "vec", None),
            P(),
            P(),
            P(LEAF_AXES),
        ),
        out_specs=P(LEAF_AXES, "vec"),
        check_vma=False,
    )
```

```python
import jax
import jax.numpy as jnp
from jax import lax
from jax.experimental import pallas as pl
from jax.experimental.pallas import tpu as pltpu
from jax.sharding import Mesh
from jax.sharding import PartitionSpec as P

LEAF = 512
RANK = 256
NEAR = 5
FAR_LEAF = 8
FAR_MID = 8
FAR_ROOT = 8
NZ = 8
NX = 4
NY = 4
LEAF_AXES = ("leaf_0", "leaf_1", "leaf_2")
RING_AXES = ("leaf_0", "leaf_2")
BF16 = jnp.bfloat16
F32 = jnp.float32


def dot(a, b):
    return jnp.dot(a, b, preferred_element_type=F32)


def swap_cores(x):
    return lax.ppermute(x, "leaf_2", [(0, 1), (1, 0)])


def ring_z(x):
    perm = []
    for z in range(NZ):
        perm.append((2 * z, 2 * ((z + 1) % NZ)))
        perm.append((2 * z + 1, 2 * ((z - 1) % NZ) + 1))
    return lax.ppermute(x, RING_AXES, perm)


def ring_y(x, step=1):
    perm = []
    for y in range(NY):
        perm.append((y, (y + step) % NY))
        perm.append((NY + y, NY + (y - step) % NY))
    return lax.ppermute(x, ("leaf_2", "vec"), perm)


def shift_x(x, step):
    return lax.ppermute(x, "leaf_1", [(i, (i + step) % NX) for i in range(NX)])


def outer_halo(x):
    count = NZ * NX * 2
    perm = []
    for p in range(count):
        target = p + 1 if p % 2 else p - 1
        if 0 <= target < count:
            perm.append((p, target))
    return lax.ppermute(x, LEAF_AXES, perm)


UNROLL = 4
MIB = 1 << 20


def hbm(*arrays):
    return [pltpu.with_memory_space_constraint(a, pltpu.HBM) for a in arrays]


def vmem(*arrays):
    return [pltpu.with_memory_space_constraint(a, pltpu.VMEM) for a in arrays]


def params(mib):
    return pltpu.CompilerParams(vmem_limit_bytes=mib * MIB)


def lists_body(owners, picks, *refs):
    kinds, (leaf, high, leaf_base, high_base) = refs[:NX], refs[NX:]
    z, x, core = (lax.axis_index(axis) for axis in LEAF_AXES)

    def base(o, _):
        dz = ((o >> 3) - z) & 7
        dist = jnp.where(core == 1, dz, (0 - dz) & 7)
        other = (o & 1) ^ core
        reach = jnp.where(other == 0, 5, 4)
        least = jnp.where(other == 0, 0, 1)
        held = (((o >> 1) & 3) == x) & (dist >= least) & (dist < reach)
        leaf_base[o] = jnp.where(held, (8 * dist + 4 * other) << 4, -4096)
        high_base[o] = jnp.where(held, (7 * dist + 4 * other) << 4, -4096)
        return 0

    lax.fori_loop(0, 64, base, 0, unroll=8)
    rows = 4 * FAR_LEAF + 2 * FAR_MID + FAR_ROOT

    def gather(bases, out, first, nodes, leaves):
        count = jnp.int32(0)
        for s in range(NX):
            tx = (x - s) & 3
            for b in range(2):
                start = (z * 8 + tx * 2 + (core ^ b)) * rows + first
                group = 4 * (tx + 4 * b)

                def node(n, count):
                    low = 3 if leaves else jnp.where(n < 2, 1, 0)
                    extra = 0 if leaves else jnp.where(n < 2, 0, 32)
                    target = (group + n) * 1024 + extra
                    for j in range(8):
                        at = bases[owners[0, start + 8 * n + j]]
                        pick = (picks[start + 8 * n + j] & low) << 4
                        out[count] = at + pick + (target + kinds[s][b, first + 8 * n + j])
                        count = count + 1 + (at >> 31)
                    return count

                count = lax.fori_loop(0, nodes, node, count)
        for u in range(UNROLL):
            out[count + u] = 32 * 1024
        out[out.shape[0] - 1] = count

    gather(leaf_base, leaf, 0, 4, True)
    gather(high_base, high, 4 * FAR_LEAF, 3, False)


def pair_lists(owners, picks, *kinds):
    smem = pl.BlockSpec(memory_space=pltpu.SMEM)
    return pl.pallas_call(
        lists_body,
        out_shape=(
            jax.ShapeDtypeStruct((384,), jnp.int32),
            jax.ShapeDtypeStruct((256,), jnp.int32),
        ),
        in_specs=[smem] * (2 + NX),
        out_specs=(smem, smem),
        scratch_shapes=[pltpu.SMEM((64,), jnp.int32)] * 2,
        compiler_params=params(1),
        name="lists",
    )(*hbm(owners, picks), *kinds)


def couple_body(high, listed, coup, *refs):
    ring, (mine, sib, buf, acc, sem) = refs[:-5], refs[-5:]
    copies, start = [], 0
    for i, r in enumerate(ring):
        size = r.shape[0]
        copies.append(pltpu.make_async_copy(r, buf.at[start : start + size], sem.at[i]))
        start += size
    for c in copies:
        c.start()
    count = listed[listed.shape[0] - 1]

    def zero(i, _):
        acc[i] = jnp.zeros((RANK, acc.shape[2]), F32)
        return 0

    lax.fori_loop(0, 33, zero, 0)
    for c in copies:
        c.wait()

    def step(g, _):
        where, parts = [], []
        for u in range(UNROLL):
            e = listed[g * UNROLL + u]
            where.append(e >> 10)
            parts.append(dot(coup[e & 15], buf[(e >> 4) & 63]))
        for t, part in zip(where, parts):
            acc[t] += part
        return 0

    lax.fori_loop(0, (count + UNROLL - 1) // UNROLL, step, 0)
    if high:
        top = buf[10].astype(F32) + buf[17].astype(F32) + buf[24].astype(F32)
        ends = buf[3].astype(F32) + buf[31].astype(F32)
        acc[3] = jnp.where(lax.axis_index("leaf_2") == 0, top + ends, top)
        for g in range(1, 8):
            acc[4 * g + 3] = acc[3]

    def out(i, _):
        mine[i] = acc[i].astype(BF16)
        sib[i] = acc[16 + i].astype(BF16)
        return 0

    lax.fori_loop(0, 16, out, 0)


def couple(high, listed, coup, *ring):
    width = ring[0].shape[-1]
    slots = sum(r.shape[0] for r in ring)
    any_spec = pl.BlockSpec(memory_space=pl.ANY)
    here = pl.BlockSpec(memory_space=pltpu.VMEM)
    smem = pl.BlockSpec(memory_space=pltpu.SMEM)

    def couple_kernel(*refs):
        couple_body(high, *refs)

    return pl.pallas_call(
        couple_kernel,
        out_shape=(jax.ShapeDtypeStruct((16, RANK, width), BF16),) * 2,
        in_specs=[smem, here] + [any_spec] * len(ring),
        out_specs=(here,) * 2,
        scratch_shapes=[
            pltpu.VMEM((slots, RANK, width), BF16),
            pltpu.VMEM((33, RANK, width), F32),
            pltpu.SemaphoreType.DMA((len(ring),)),
        ],
        compiler_params=params(12),
        name="couple_high" if high else "couple_leaf",
    )(*vmem(listed, coup, *ring))


def near_body(blocks_hbm, *refs):
    chunks, outs, (buf, blocks, sem) = refs[:4], refs[4:8], refs[8:]
    copies = []
    for k in range(4):
        there = buf.at[:, 128 * k : 128 * (k + 1)]
        copies.append(pltpu.make_async_copy(chunks[k], there, sem.at[k]))
    for i in range(4):
        copies.append(pltpu.make_async_copy(blocks_hbm.at[i], blocks.at[i], sem.at[4 + i]))
    for c in copies:
        c.start()
    for c in copies:
        c.wait()

    def leaf(i, _):
        total = jnp.zeros((128, 512), F32)
        for b in range(NEAR):
            rows = pl.ds(pl.multiple_of((i + b) * LEAF, LEAF), LEAF)
            total += dot(blocks[i, b], buf[rows])
        for k in range(4):
            outs[k][i] = total[:, 128 * k : 128 * (k + 1)].astype(BF16)
        return 0

    lax.fori_loop(0, 4, leaf, 0)


def near_products(blocks, *chunks):
    any_spec = pl.BlockSpec(memory_space=pl.ANY)
    here = pl.BlockSpec(memory_space=pltpu.VMEM)
    return pl.pallas_call(
        near_body,
        out_shape=(jax.ShapeDtypeStruct((4, 128, 128), BF16),) * 4,
        in_specs=[any_spec] * 5,
        out_specs=(here,) * 4,
        scratch_shapes=[
            pltpu.VMEM((4096, 512), BF16),
            pltpu.VMEM(blocks.shape, BF16),
            pltpu.SemaphoreType.DMA((8,)),
        ],
        compiler_params=params(10),
        name="near",
    )(*hbm(blocks), *vmem(*chunks))


def tail_body(*refs):
    part_l, part_h, near, weights, out = refs[:4], refs[4:8], refs[8:12], refs[12:17], refs[17]
    nbuf, held, sem = refs[18], refs[19:24], refs[24]
    copies = []
    for i in range(5):
        copies.append(pltpu.make_async_copy(weights[i], held[i], sem.at[i]))
    for c in copies:
        c.start()
    top_c, top_down, up_mid, up_leaf, basis = held
    core, y = lax.axis_index("leaf_2"), lax.axis_index("vec")
    for k in range(NY):
        nbuf[(y + jnp.where(core == 0, k, 4 - k)) & 3] = near[k][...]

    def far(part, i):
        total = part[0][i].astype(F32)
        for p in range(1, NX):
            total += part[p][i].astype(F32)
        return total

    top = far(part_h, 3).astype(BF16)
    copies[0].wait()
    top_local = dot(top_c[...], top).astype(BF16)
    copies[1].wait()
    down_root = (far(part_h, 2) + dot(top_down[0], top_local)).astype(BF16)
    for c in copies[2:]:
        c.wait()
    for m in range(2):
        down_mid = (far(part_h, m) + dot(up_mid[m], down_root)).astype(BF16)
        for k in range(2):
            i = 2 * m + k
            down_leaf = (far(part_l, i) + dot(up_leaf[i], down_mid)).astype(BF16)
            field = dot(basis[i], down_leaf)
            for v in range(NY):
                rows = field[128 * v : 128 * (v + 1)] + nbuf[v, i].astype(F32)
                out[i * LEAF + 128 * v : i * LEAF + 128 * (v + 1)] = rows.astype(BF16)


def tail(*operands):
    here, any_spec = pl.BlockSpec(memory_space=pltpu.VMEM), pl.BlockSpec(memory_space=pl.ANY)
    width = operands[0].shape[-1]
    return pl.pallas_call(
        tail_body,
        out_shape=jax.ShapeDtypeStruct((4 * LEAF, width), BF16),
        in_specs=[here] * 12 + [any_spec] * 5,
        out_specs=here,
        scratch_shapes=[pltpu.VMEM((NY, 4, 128, width), BF16)]
        + [pltpu.VMEM(w.shape, BF16) for w in operands[12:]]
        + [pltpu.SemaphoreType.DMA((5,))],
        compiler_params=params(10),
        name="tail",
    )(*vmem(*operands[:12]), *hbm(*operands[12:]))


def climb_body(leaf, up_leaf, up_mid, top_up, out):
    def lift(up, coeff):
        sides = (((0,), (0,)), ((), ()))
        return lax.dot_general(up, coeff, sides, preferred_element_type=F32)

    root = None
    for m in range(2):
        first, second = lift(up_leaf[2 * m], leaf[2 * m]), lift(up_leaf[2 * m + 1], leaf[2 * m + 1])
        out[m] = (first + second).astype(BF16)
        part = lift(up_mid[m], out[m])
        root = part if m == 0 else root + part
    out[2] = root.astype(BF16)
    out[3] = lift(top_up[0], out[2]).astype(BF16)


def climb(*operands):
    here = pl.BlockSpec(memory_space=pltpu.VMEM)
    return pl.pallas_call(
        climb_body,
        out_shape=jax.ShapeDtypeStruct(operands[0].shape, BF16),
        in_specs=[here] * 4,
        out_specs=here,
        compiler_params=params(6),
        name="climb",
    )(*vmem(operands[0]), *hbm(*operands[1:]))


def merge_body(mine, got, *outs):
    x = lax.axis_index("leaf_1")
    for g in range(NX):

        def one(i, _):
            at = 4 * ((x + g) & 3) + i
            outs[g][i] = (mine[at].astype(F32) + got[at].astype(F32)).astype(BF16)
            return 0

        lax.fori_loop(0, 4, one, 0)


def merge(mine, got):
    here = pl.BlockSpec(memory_space=pltpu.VMEM)
    return pl.pallas_call(
        merge_body,
        out_shape=(jax.ShapeDtypeStruct((4,) + mine.shape[1:], BF16),) * NX,
        in_specs=[here] * 2,
        out_specs=(here,) * NX,
        compiler_params=params(4),
        name="merge",
    )(*vmem(mine, got))


def head_body(whole, out):
    out[...] = whole[: out.shape[0]]


def first_nodes(whole, count):
    here = pl.BlockSpec(memory_space=pltpu.VMEM)
    return pl.pallas_call(
        head_body,
        out_shape=jax.ShapeDtypeStruct((count,) + whole.shape[1:], BF16),
        in_specs=[here],
        out_specs=here,
        compiler_params=params(2),
        name="first",
    )(*vmem(whole))


def pack_body(own, other, out):
    out[0:3] = own[0:3]
    out[3] = (own[3].astype(F32) + other[3].astype(F32)).astype(BF16)
    out[4:7] = other[0:3]


def join_body(own, other, out):
    out[0:4] = own[...]
    out[4:8] = other[...]


def pack_leaf(own, other):
    here = pl.BlockSpec(memory_space=pltpu.VMEM)
    return pl.pallas_call(
        join_body,
        out_shape=jax.ShapeDtypeStruct((8,) + own.shape[1:], BF16),
        in_specs=[here] * 2,
        out_specs=here,
        compiler_params=params(3),
        name="join",
    )(own, other)


def pack_high(own, other):
    here = pl.BlockSpec(memory_space=pltpu.VMEM)
    return pl.pallas_call(
        pack_body,
        out_shape=jax.ShapeDtypeStruct((7,) + own.shape[1:], BF16),
        in_specs=[here] * 2,
        out_specs=here,
        compiler_params=params(3),
        name="pack",
    )(own, other)


def widen_body(middle, halo, sib, out, sem):
    core = lax.axis_index("leaf_2")
    copies = [
        pltpu.make_async_copy(middle, out.at[1024:3072], sem.at[0]),
        pltpu.make_async_copy(halo, out.at[pl.ds(core * 3072, 1024)], sem.at[1]),
        pltpu.make_async_copy(sib, out.at[pl.ds((1 - core) * 3072, 1024)], sem.at[2]),
    ]
    for c in copies:
        c.start()
    for c in copies:
        c.wait()


def widen(middle, halo, sib):
    any_spec = pl.BlockSpec(memory_space=pl.ANY)
    return pl.pallas_call(
        widen_body,
        out_shape=jax.ShapeDtypeStruct((4096, middle.shape[1]), BF16),
        in_specs=[any_spec] * 3,
        out_specs=pl.BlockSpec(memory_space=pltpu.VMEM),
        scratch_shapes=[pltpu.SemaphoreType.DMA((3,))],
        compiler_params=params(3),
        name="widen",
    )(middle, halo, sib)


def exchange(mine, sib):
    got = swap_cores(sib)
    totals = list(merge(mine, got))
    for g in (2, 1, 3):
        totals[g] = shift_x(totals[g], g)
    return totals


def body(
    vectors,
    leaf_basis,
    up_leaf,
    up_mid,
    top_up,
    top_down,
    couplings,
    coupling_top,
    near_blocks,
    far_owner,
    far_pick,
    far_kind,
):
    core = lax.axis_index("leaf_2")
    width = vectors.shape[1]
    far_rows = far_kind.shape[0]

    coeff_leaf = jnp.einsum(
        "nlr,nlv->nrv", leaf_basis, vectors.reshape(4, LEAF, width), preferred_element_type=F32
    ).astype(BF16)
    coeff_high = climb(coeff_leaf, up_leaf, up_mid, top_up)

    other_l = swap_cores(coeff_leaf)
    other_h = swap_cores(coeff_high)
    ring_l = [pack_leaf(coeff_leaf, other_l)]
    for _ in range(1, 4):
        ring_l.append(ring_z(ring_l[-1]))
    ring_l.append(ring_z(first_nodes(ring_l[-1], 4)))
    ring_h = [pack_high(coeff_high, other_h)]
    for _ in range(1, 4):
        ring_h.append(ring_z(ring_h[-1]))
    ring_h.append(ring_z(first_nodes(ring_h[-1], 4)))

    upper = core == 0
    outer = jnp.where(upper, vectors[:1024], vectors[1024:])
    inner = jnp.where(upper, vectors[1024:], vectors[:1024])
    halo = outer_halo(outer)
    sib = swap_cores(inner)
    chunks = [widen(vectors, halo, sib)]
    for _ in range(1, NY):
        chunks.append(ring_y(chunks[-1]))

    kinds = far_kind.reshape(1, far_rows)
    kinds = [jnp.concatenate([kinds, swap_cores(kinds)], axis=0)]
    for k in range(1, NX):
        kinds.append(shift_x(kinds[0], k))
    operands = (far_owner.reshape(1, -1), far_pick, *kinds)
    leaf_list, high_list = pair_lists(*operands)

    sums_l = couple(False, leaf_list, couplings, *ring_l)
    sums_h = couple(True, high_list, couplings, *ring_h)
    part_l = exchange(*sums_l)
    part_h = exchange(*sums_h)

    near = list(near_products(near_blocks, *chunks))
    for k in range(1, NY):
        near[k] = ring_y(near[k], -k)

    return tail(*part_l, *part_h, *near, coupling_top, top_down, up_mid, up_leaf, leaf_basis)


def solution(mesh):
    torus = Mesh(mesh.devices.reshape(NZ, NX, 2, NY), LEAF_AXES + ("vec",))

    return jax.shard_map(
        body,
        mesh=torus,
        in_specs=(
            P(LEAF_AXES, "vec"),
            P(LEAF_AXES, None, None),
            P(LEAF_AXES, None, None),
            P(LEAF_AXES, None, None),
            P(LEAF_AXES, None, None),
            P(LEAF_AXES, None, None),
            P(),
            P(),
            P(LEAF_AXES, None, "vec", None),
            P(),
            P(),
            P(LEAF_AXES),
        ),
        out_specs=P(LEAF_AXES, "vec"),
        check_vma=False,
    )
```

```python
import jax
import jax.numpy as jnp
from jax import lax
from jax.experimental import pallas as pl
from jax.experimental.pallas import tpu as pltpu
from jax.sharding import Mesh
from jax.sharding import PartitionSpec as P

LEAF = 512
RANK = 256
NEAR = 5
FAR_LEAF = 8
FAR_MID = 8
FAR_ROOT = 8
NZ = 8
NX = 4
NY = 4
LEAF_AXES = ("leaf_0", "leaf_1", "leaf_2")
RING_AXES = ("leaf_0", "leaf_2")
BF16 = jnp.bfloat16
F32 = jnp.float32


def dot(a, b):
    return jnp.dot(a, b, preferred_element_type=F32)


def swap_cores(x):
    return lax.ppermute(x, "leaf_2", [(0, 1), (1, 0)])


def ring_z(x):
    perm = []
    for z in range(NZ):
        perm.append((2 * z, 2 * ((z + 1) % NZ)))
        perm.append((2 * z + 1, 2 * ((z - 1) % NZ) + 1))
    return lax.ppermute(x, RING_AXES, perm)


def ring_y(x, step=1):
    perm = []
    for y in range(NY):
        perm.append((y, (y + step) % NY))
        perm.append((NY + y, NY + (y - step) % NY))
    return lax.ppermute(x, ("leaf_2", "vec"), perm)


def shift_x(x, step):
    return lax.ppermute(x, "leaf_1", [(i, (i + step) % NX) for i in range(NX)])


def outer_halo(x):
    count = NZ * NX * 2
    perm = []
    for p in range(count):
        target = p + 1 if p % 2 else p - 1
        if 0 <= target < count:
            perm.append((p, target))
    return lax.ppermute(x, LEAF_AXES, perm)


UNROLL = 4
MIB = 1 << 20


def hbm(*arrays):
    return [pltpu.with_memory_space_constraint(a, pltpu.HBM) for a in arrays]


def vmem(*arrays):
    return [pltpu.with_memory_space_constraint(a, pltpu.VMEM) for a in arrays]


def params(mib):
    return pltpu.CompilerParams(vmem_limit_bytes=mib * MIB)


def lists_body(owners, picks, *refs):
    kinds, (leaf, high, leaf_base, high_base) = refs[:NX], refs[NX:]
    z, x, core = (lax.axis_index(axis) for axis in LEAF_AXES)

    def base(o, _):
        dz = ((o >> 3) - z) & 7
        dist = jnp.where(core == 1, dz, (0 - dz) & 7)
        other = (o & 1) ^ core
        reach = jnp.where(other == 0, 5, 4)
        least = jnp.where(other == 0, 0, 1)
        held = (((o >> 1) & 3) == x) & (dist >= least) & (dist < reach)
        leaf_base[o] = jnp.where(held, (8 * dist + 4 * other) << 4, -4096)
        high_base[o] = jnp.where(held, (7 * dist + 4 * other) << 4, -4096)
        return 0

    lax.fori_loop(0, 64, base, 0, unroll=8)
    rows = 4 * FAR_LEAF + 2 * FAR_MID + FAR_ROOT

    def gather(bases, out, first, nodes, leaves):
        count = jnp.int32(0)
        for s in range(NX):
            tx = (x - s) & 3
            for b in range(2):
                start = (z * 8 + tx * 2 + (core ^ b)) * rows + first
                group = 4 * (tx + 4 * b)

                def node(n, count):
                    low = 3 if leaves else jnp.where(n < 2, 1, 0)
                    extra = 0 if leaves else jnp.where(n < 2, 0, 32)
                    target = (group + n) * 1024 + extra
                    for j in range(8):
                        at = bases[owners[0, start + 8 * n + j]]
                        pick = (picks[start + 8 * n + j] & low) << 4
                        out[count] = at + pick + (target + kinds[s][b, first + 8 * n + j])
                        count = count + 1 + (at >> 31)
                    return count

                count = lax.fori_loop(0, nodes, node, count)
        for u in range(UNROLL):
            out[count + u] = 32 * 1024
        out[out.shape[0] - 1] = count

    gather(leaf_base, leaf, 0, 4, True)
    gather(high_base, high, 4 * FAR_LEAF, 3, False)


def pair_lists(owners, picks, *kinds):
    smem = pl.BlockSpec(memory_space=pltpu.SMEM)
    return pl.pallas_call(
        lists_body,
        out_shape=(
            jax.ShapeDtypeStruct((384,), jnp.int32),
            jax.ShapeDtypeStruct((256,), jnp.int32),
        ),
        in_specs=[smem] * (2 + NX),
        out_specs=(smem, smem),
        scratch_shapes=[pltpu.SMEM((64,), jnp.int32)] * 2,
        compiler_params=params(1),
        name="lists",
    )(*hbm(owners, picks), *kinds)


def couple_body(high, listed, coup, *refs):
    ring, (mine, sib, buf, acc, sem) = refs[:-5], refs[-5:]
    copies, start = [], 0
    for i, r in enumerate(ring):
        size = r.shape[0]
        copies.append(pltpu.make_async_copy(r, buf.at[start : start + size], sem.at[i]))
        start += size
    for c in copies:
        c.start()
    count = listed[listed.shape[0] - 1]

    def zero(i, _):
        acc[i] = jnp.zeros((RANK, acc.shape[2]), F32)
        return 0

    lax.fori_loop(0, 33, zero, 0)
    for c in copies:
        c.wait()

    def step(g, _):
        where, parts = [], []
        for u in range(UNROLL):
            e = listed[g * UNROLL + u]
            where.append(e >> 10)
            parts.append(dot(coup[e & 15], buf[(e >> 4) & 63]))
        for t, part in zip(where, parts):
            acc[t] += part
        return 0

    lax.fori_loop(0, (count + UNROLL - 1) // UNROLL, step, 0)
    if high:
        top = buf[10].astype(F32) + buf[17].astype(F32) + buf[24].astype(F32)
        ends = buf[3].astype(F32) + buf[31].astype(F32)
        acc[3] = jnp.where(lax.axis_index("leaf_2") == 0, top + ends, top)
        for g in range(1, 8):
            acc[4 * g + 3] = acc[3]

    def out(i, _):
        mine[i] = acc[i].astype(BF16)
        sib[i] = acc[16 + i].astype(BF16)
        return 0

    lax.fori_loop(0, 16, out, 0)


def couple(high, listed, coup, *ring):
    width = ring[0].shape[-1]
    slots = sum(r.shape[0] for r in ring)
    any_spec = pl.BlockSpec(memory_space=pl.ANY)
    here = pl.BlockSpec(memory_space=pltpu.VMEM)
    smem = pl.BlockSpec(memory_space=pltpu.SMEM)

    def couple_kernel(*refs):
        couple_body(high, *refs)

    return pl.pallas_call(
        couple_kernel,
        out_shape=(jax.ShapeDtypeStruct((16, RANK, width), BF16),) * 2,
        in_specs=[smem, here] + [any_spec] * len(ring),
        out_specs=(here,) * 2,
        scratch_shapes=[
            pltpu.VMEM((slots, RANK, width), BF16),
            pltpu.VMEM((33, RANK, width), F32),
            pltpu.SemaphoreType.DMA((len(ring),)),
        ],
        compiler_params=params(12),
        name="couple_high" if high else "couple_leaf",
    )(*vmem(listed, coup, *ring))


def near_body(blocks_hbm, *refs):
    chunks, outs, (buf, blocks, sem) = refs[:4], refs[4:8], refs[8:]
    copies = []
    for k in range(4):
        there = buf.at[:, 128 * k : 128 * (k + 1)]
        copies.append(pltpu.make_async_copy(chunks[k], there, sem.at[k]))
    for i in range(4):
        copies.append(pltpu.make_async_copy(blocks_hbm.at[i], blocks.at[i], sem.at[4 + i]))
    for c in copies:
        c.start()
    for c in copies[:4]:
        c.wait()
    for i in range(4):
        copies[4 + i].wait()
        total = dot(blocks[i, 0], buf[i * LEAF : (i + 1) * LEAF])
        for b in range(1, NEAR):
            total += dot(blocks[i, b], buf[(i + b) * LEAF : (i + b + 1) * LEAF])
        for k in range(4):
            outs[k][i] = total[:, 128 * k : 128 * (k + 1)].astype(BF16)


def near_products(blocks, *chunks):
    any_spec = pl.BlockSpec(memory_space=pl.ANY)
    here = pl.BlockSpec(memory_space=pltpu.VMEM)
    return pl.pallas_call(
        near_body,
        out_shape=(jax.ShapeDtypeStruct((4, 128, 128), BF16),) * 4,
        in_specs=[any_spec] * 5,
        out_specs=(here,) * 4,
        scratch_shapes=[
            pltpu.VMEM((4096, 512), BF16),
            pltpu.VMEM(blocks.shape, BF16),
            pltpu.SemaphoreType.DMA((8,)),
        ],
        compiler_params=params(10),
        name="near",
    )(*hbm(blocks), *vmem(*chunks))


def tail_body(*refs):
    part_l, part_h, near, weights, out = refs[:4], refs[4:8], refs[8:12], refs[12:17], refs[17]
    nbuf, held, sem = refs[18], refs[19:24], refs[24]
    copies = []
    for i in range(5):
        copies.append(pltpu.make_async_copy(weights[i], held[i], sem.at[i]))
    for c in copies:
        c.start()
    top_c, top_down, up_mid, up_leaf, basis = held
    core, y = lax.axis_index("leaf_2"), lax.axis_index("vec")
    for k in range(NY):
        nbuf[(y + jnp.where(core == 0, k, 4 - k)) & 3] = near[k][...]

    def far(part, i):
        total = part[0][i].astype(F32)
        for p in range(1, NX):
            total += part[p][i].astype(F32)
        return total

    top = far(part_h, 3).astype(BF16)
    copies[0].wait()
    top_local = dot(top_c[...], top).astype(BF16)
    copies[1].wait()
    down_root = (far(part_h, 2) + dot(top_down[0], top_local)).astype(BF16)
    for c in copies[2:]:
        c.wait()
    for m in range(2):
        down_mid = (far(part_h, m) + dot(up_mid[m], down_root)).astype(BF16)
        for k in range(2):
            i = 2 * m + k
            down_leaf = (far(part_l, i) + dot(up_leaf[i], down_mid)).astype(BF16)
            field = dot(basis[i], down_leaf)
            for v in range(NY):
                rows = field[128 * v : 128 * (v + 1)] + nbuf[v, i].astype(F32)
                out[i * LEAF + 128 * v : i * LEAF + 128 * (v + 1)] = rows.astype(BF16)


def tail(*operands):
    here, any_spec = pl.BlockSpec(memory_space=pltpu.VMEM), pl.BlockSpec(memory_space=pl.ANY)
    width = operands[0].shape[-1]
    return pl.pallas_call(
        tail_body,
        out_shape=jax.ShapeDtypeStruct((4 * LEAF, width), BF16),
        in_specs=[here] * 12 + [any_spec] * 5,
        out_specs=here,
        scratch_shapes=[pltpu.VMEM((NY, 4, 128, width), BF16)]
        + [pltpu.VMEM(w.shape, BF16) for w in operands[12:]]
        + [pltpu.SemaphoreType.DMA((5,))],
        compiler_params=params(10),
        name="tail",
    )(*vmem(*operands[:12]), *hbm(*operands[12:]))


def climb_body(leaf, up_leaf, up_mid, top_up, out):
    def lift(up, coeff):
        sides = (((0,), (0,)), ((), ()))
        return lax.dot_general(up, coeff, sides, preferred_element_type=F32)

    root = None
    for m in range(2):
        first, second = lift(up_leaf[2 * m], leaf[2 * m]), lift(up_leaf[2 * m + 1], leaf[2 * m + 1])
        out[m] = (first + second).astype(BF16)
        part = lift(up_mid[m], out[m])
        root = part if m == 0 else root + part
    out[2] = root.astype(BF16)
    out[3] = lift(top_up[0], out[2]).astype(BF16)


def climb(*operands):
    here = pl.BlockSpec(memory_space=pltpu.VMEM)
    return pl.pallas_call(
        climb_body,
        out_shape=jax.ShapeDtypeStruct(operands[0].shape, BF16),
        in_specs=[here] * 4,
        out_specs=here,
        compiler_params=params(6),
        name="climb",
    )(*vmem(operands[0]), *hbm(*operands[1:]))


def merge_body(mine, got, *outs):
    x = lax.axis_index("leaf_1")
    for g in range(NX):

        def one(i, _):
            at = 4 * ((x + g) & 3) + i
            outs[g][i] = (mine[at].astype(F32) + got[at].astype(F32)).astype(BF16)
            return 0

        lax.fori_loop(0, 4, one, 0)


def merge(mine, got):
    here = pl.BlockSpec(memory_space=pltpu.VMEM)
    return pl.pallas_call(
        merge_body,
        out_shape=(jax.ShapeDtypeStruct((4,) + mine.shape[1:], BF16),) * NX,
        in_specs=[here] * 2,
        out_specs=(here,) * NX,
        compiler_params=params(4),
        name="merge",
    )(*vmem(mine, got))


def head_body(whole, out):
    out[...] = whole[: out.shape[0]]


def first_nodes(whole, count):
    here = pl.BlockSpec(memory_space=pltpu.VMEM)
    return pl.pallas_call(
        head_body,
        out_shape=jax.ShapeDtypeStruct((count,) + whole.shape[1:], BF16),
        in_specs=[here],
        out_specs=here,
        compiler_params=params(2),
        name="first",
    )(*vmem(whole))


def pack_body(own, other, out):
    out[0:3] = own[0:3]
    out[3] = (own[3].astype(F32) + other[3].astype(F32)).astype(BF16)
    out[4:7] = other[0:3]


def join_body(own, other, out):
    out[0:4] = own[...]
    out[4:8] = other[...]


def pack_leaf(own, other):
    here = pl.BlockSpec(memory_space=pltpu.VMEM)
    return pl.pallas_call(
        join_body,
        out_shape=jax.ShapeDtypeStruct((8,) + own.shape[1:], BF16),
        in_specs=[here] * 2,
        out_specs=here,
        compiler_params=params(3),
        name="join",
    )(own, other)


def pack_high(own, other):
    here = pl.BlockSpec(memory_space=pltpu.VMEM)
    return pl.pallas_call(
        pack_body,
        out_shape=jax.ShapeDtypeStruct((7,) + own.shape[1:], BF16),
        in_specs=[here] * 2,
        out_specs=here,
        compiler_params=params(3),
        name="pack",
    )(own, other)


def widen_body(middle, halo, sib, out, sem):
    core = lax.axis_index("leaf_2")
    copies = [
        pltpu.make_async_copy(middle, out.at[1024:3072], sem.at[0]),
        pltpu.make_async_copy(halo, out.at[pl.ds(core * 3072, 1024)], sem.at[1]),
        pltpu.make_async_copy(sib, out.at[pl.ds((1 - core) * 3072, 1024)], sem.at[2]),
    ]
    for c in copies:
        c.start()
    for c in copies:
        c.wait()


def widen(middle, halo, sib):
    any_spec = pl.BlockSpec(memory_space=pl.ANY)
    return pl.pallas_call(
        widen_body,
        out_shape=jax.ShapeDtypeStruct((4096, middle.shape[1]), BF16),
        in_specs=[any_spec] * 3,
        out_specs=pl.BlockSpec(memory_space=pltpu.VMEM),
        scratch_shapes=[pltpu.SemaphoreType.DMA((3,))],
        compiler_params=params(3),
        name="widen",
    )(middle, halo, sib)


def exchange(mine, sib):
    got = swap_cores(sib)
    totals = list(merge(mine, got))
    for g in (2, 1, 3):
        totals[g] = shift_x(totals[g], g)
    return totals


def body(
    vectors,
    leaf_basis,
    up_leaf,
    up_mid,
    top_up,
    top_down,
    couplings,
    coupling_top,
    near_blocks,
    far_owner,
    far_pick,
    far_kind,
):
    core = lax.axis_index("leaf_2")
    width = vectors.shape[1]
    far_rows = far_kind.shape[0]

    coeff_leaf = jnp.einsum(
        "nlr,nlv->nrv", leaf_basis, vectors.reshape(4, LEAF, width), preferred_element_type=F32
    ).astype(BF16)
    coeff_high = climb(coeff_leaf, up_leaf, up_mid, top_up)

    other_l = swap_cores(coeff_leaf)
    other_h = swap_cores(coeff_high)
    ring_l = [pack_leaf(coeff_leaf, other_l)]
    for _ in range(1, 4):
        ring_l.append(ring_z(ring_l[-1]))
    ring_l.append(ring_z(first_nodes(ring_l[-1], 4)))
    ring_h = [pack_high(coeff_high, other_h)]
    for _ in range(1, 4):
        ring_h.append(ring_z(ring_h[-1]))
    ring_h.append(ring_z(first_nodes(ring_h[-1], 4)))

    upper = core == 0
    outer = jnp.where(upper, vectors[:1024], vectors[1024:])
    inner = jnp.where(upper, vectors[1024:], vectors[:1024])
    halo = outer_halo(outer)
    sib = swap_cores(inner)
    chunks = [widen(vectors, halo, sib)]
    for _ in range(1, NY):
        chunks.append(ring_y(chunks[-1]))

    kinds = far_kind.reshape(1, far_rows)
    kinds = [jnp.concatenate([kinds, swap_cores(kinds)], axis=0)]
    for k in range(1, NX):
        kinds.append(shift_x(kinds[0], k))
    operands = (far_owner.reshape(1, -1), far_pick, *kinds)
    leaf_list, high_list = pair_lists(*operands)

    sums_l = couple(False, leaf_list, couplings, *ring_l)
    sums_h = couple(True, high_list, couplings, *ring_h)
    part_l = exchange(*sums_l)
    part_h = exchange(*sums_h)

    near = list(near_products(near_blocks, *chunks))
    for k in range(1, NY):
        near[k] = ring_y(near[k], -k)

    return tail(*part_l, *part_h, *near, coupling_top, top_down, up_mid, up_leaf, leaf_basis)


def solution(mesh):
    torus = Mesh(mesh.devices.reshape(NZ, NX, 2, NY), LEAF_AXES + ("vec",))

    return jax.shard_map(
        body,
        mesh=torus,
        in_specs=(
            P(LEAF_AXES, "vec"),
            P(LEAF_AXES, None, None),
            P(LEAF_AXES, None, None),
            P(LEAF_AXES, None, None),
            P(LEAF_AXES, None, None),
            P(LEAF_AXES, None, None),
            P(),
            P(),
            P(LEAF_AXES, None, "vec", None),
            P(),
            P(),
            P(LEAF_AXES),
        ),
        out_specs=P(LEAF_AXES, "vec"),
        check_vma=False,
    )
```
